768 devices in a mesh: tm: 24 (over z, x_hi), space: 32 (over x_lo, y, core).
Axes of the slice: x: 4 (x_hi: 2, x_lo: 2; x = x_hi * 2 + x_lo), y: 8, z: 12, core: 2. Of those that a mesh axis runs over, the one named last changes fastest.
Arguments:
- noise_field: float32 [8, 24, 32, 6, 256], P(None, 'tm', 'space'), may hold values from -6 to 6
- gauge_links: float32 [4, 3, 24, 32, 6, 256], P(None, None, 'tm', 'space'), may hold values from -2.5 to 2.5
- clover: float32 [2, 6, 24, 32, 12, 256], P(None, None, 'tm', 'space'), may hold values from -0.9 to 0.9
- eigvecs: float32 [48, 24, 32, 6, 256], P(None, 'tm', 'space'), may hold values from -0.02734375 to 0.02734375
- partner: int32 [48], replicated, may hold values from 0 to 47, each once
- dilution: int32 [8], replicated, may hold values from 0 to 3
- boundary: int32 [4], replicated, may hold values from 0 to 1
Outputs:
- perambulator: float32 [32, 24, 96], P('space', 'tm')
- correlator: float32 [32, 24, 24], P('space', 'tm')
The draws below stay inside these ranges and needn't reach their ends.
Inputs may be any that keep to these rules, and one draw needn't show every extreme that they name: `partner`: each of 0 to 47 once.
All inputs are finite; a program needn't handle non-finite values.
Results may differ from the reference program's by a relative error of at most 0.00029.
Values sent between devices are 32-bit elements; how exact they have to be, the bound alone decides.
No kernel may reach another device: no remote copies, remote signals or barrier semaphores. Data moves between devices by JAX's collectives and lax.ppermute only.
A program may use at most 64 MiB of HBM per device.

```python
import jax
import jax.numpy as jnp
from jax import lax

NEV = 48
NSRC = 8
ITERS = 4
DILUTE = 4
SIDE = 16
LZ = 1
NT = 24
NZ = 32
N_SPACE = 32


def with_ends(entries, stream_key, low, high):
    shape = entries.shape
    index_at = [jax.random.randint(jax.random.fold_in(stream_key, axis), (), 0, shape[axis]) for axis in range(len(shape))]
    entries = entries.at[tuple(index_at)].set(low)
    longest = shape.index(max(shape))
    index_at[longest] = (index_at[longest] + 1) % shape[longest]
    return entries.at[tuple(index_at)].set(high)


def levels(stream_key, shape, cuts, least, top_value):
    def one(dim, shards_of):
        draws = jax.random.uniform(jax.random.fold_in(jax.random.fold_in(stream_key, 6), dim), (shards_of,), jnp.float32, least / len(cuts), top_value / len(cuts))
        return jnp.repeat(jnp.exp(draws), shape[dim] // shards_of).reshape((-1,) + (1,) * (len(shape) - dim - 1))

    gain = one(*cuts[0])
    for cut in cuts[1:]:
        gain = gain * one(*cut)
    return gain


def bell_draw(rng, shape, width, most, cuts=(), kind=jnp.bfloat16):
    values = width * jax.random.normal(rng, shape, jnp.float32)
    if cuts:
        values = values * levels(rng, shape, cuts, -0.22, 0.18)
    return jnp.clip(values, -most, most).astype(kind)


def setup_inputs(seed: int = 0) -> dict:
    key_list = jax.random.split(jax.random.key(seed), 8)
    noise_field = bell_draw(key_list[0], (NSRC, NT, NZ, 6, SIDE * SIDE), 1.0, 6.0, ((1, 24), (2, 32)), jnp.float32)
    gauge_links = bell_draw(key_list[1], (4, 3, NT, NZ, 6, SIDE * SIDE), 6 ** -0.5, 2.5, ((2, 24), (3, 32)), jnp.float32)
    clover = bell_draw(key_list[2], (2, 6, NT, NZ, 12, SIDE * SIDE), 0.15, 0.9, ((2, 24), (3, 32)), jnp.float32)
    eigvecs = bell_draw(key_list[3], (NEV, NT, NZ, 6, SIDE * SIDE), (6 * SIDE * SIDE * LZ * N_SPACE) ** -0.5, 0.02734375, ((1, 24), (2, 32)), jnp.float32)
    partner = jax.random.permutation(key_list[4], NEV).astype(jnp.int32)
    dilution = with_ends(jax.random.randint(key_list[5], (NSRC,), 0, DILUTE), jax.random.fold_in(key_list[5], 1), 0, DILUTE - 1).astype(jnp.int32)
    boundary = with_ends(jax.random.randint(key_list[6], (4,), 0, 2), jax.random.fold_in(key_list[6], 1), 0, 1).astype(jnp.int32)
    return {"noise_field": noise_field, "gauge_links": gauge_links, "clover": clover, "eigvecs": eigvecs, "partner": partner, "dilution": dilution, "boundary": boundary}


diag_term = 4.1
step_size = 0.2
twist_table = (
    (((1, 0, -1), (0, 0, -1)), ((1, 0, 1), (0, 0, 1))),
    (((1, -1, 0), (0, 1, 0)), ((1, 1, 0), (0, -1, 0))),
    (((0, 0, -1), (1, 0, 1)), ((0, 0, 1), (1, 0, -1))),
    (((0, 1, 0), (1, 1, 0)), ((0, 1, 0), (1, 1, 0))),
)


def pair_add(first_pair, second_pair):
    return (first_pair[0] + second_pair[0], first_pair[1] + second_pair[1])


def pair_sub(first_pair, second_pair):
    return (first_pair[0] - second_pair[0], first_pair[1] - second_pair[1])


def pair_scale(factor, value_pair):
    return (factor * value_pair[0], factor * value_pair[1])


def scaled(value_pair, real_coef, imag_coef):
    if imag_coef == 0:
        return (real_coef * value_pair[0], real_coef * value_pair[1])
    return (-imag_coef * value_pair[1], imag_coef * value_pair[0])


def spin_twist(direction, adjoint, half_pair):
    outputs = []
    for source_spin, real_coef, imag_coef in twist_table[direction][adjoint]:
        picked = (half_pair[0][:, source_spin], half_pair[1][:, source_spin])
        outputs.append(scaled(picked, real_coef, imag_coef))
    return (jnp.stack([outputs[0][0], outputs[1][0]], 1), jnp.stack([outputs[0][1], outputs[1][1]], 1))


def split_spins(spinor_pair):
    upper_half = (spinor_pair[0][:, 0:2], spinor_pair[1][:, 0:2])
    lower_half = (spinor_pair[0][:, 2:4], spinor_pair[1][:, 2:4])
    return upper_half, lower_half


def link_apply(link_real, link_imag, half_pair):
    total_real = 0.0
    total_imag = 0.0
    for column in range(3):
        matrix_real = jnp.moveaxis(link_real[:, :, :, column, :], 0, 2)
        matrix_imag = jnp.moveaxis(link_imag[:, :, :, column, :], 0, 2)
        vector_real = half_pair[0][..., column:column + 1, :]
        vector_imag = half_pair[1][..., column:column + 1, :]
        total_real = total_real + matrix_real * vector_real - matrix_imag * vector_imag
        total_imag = total_imag + matrix_real * vector_imag + matrix_imag * vector_real
    return (total_real, total_imag)


def link_adjoint(link_real, link_imag, half_pair):
    total_real = 0.0
    total_imag = 0.0
    for matrix_row in range(3):
        matrix_real = link_real[matrix_row]
        matrix_imag = link_imag[matrix_row]
        vector_real = half_pair[0][..., matrix_row:matrix_row + 1, :]
        vector_imag = half_pair[1][..., matrix_row:matrix_row + 1, :]
        total_real = total_real + matrix_real * vector_real + matrix_imag * vector_imag
        total_imag = total_imag + matrix_real * vector_imag - matrix_imag * vector_real
    return (total_real, total_imag)


def plane_shift(values, direction, forward, edge_sign):
    flat_index = lax.broadcasted_iota(jnp.int32, values.shape, values.ndim - 1)
    if direction == 0:
        coordinate = flat_index % SIDE
        if forward:
            return jnp.where(coordinate == SIDE - 1, edge_sign * jnp.roll(values, SIDE - 1, axis=-1), jnp.roll(values, -1, axis=-1))
        return jnp.where(coordinate == 0, edge_sign * jnp.roll(values, 1 - SIDE, axis=-1), jnp.roll(values, 1, axis=-1))
    coordinate = flat_index // SIDE
    if forward:
        rolled = jnp.roll(values, -SIDE, axis=-1)
        return jnp.where(coordinate == SIDE - 1, edge_sign * rolled, rolled)
    rolled = jnp.roll(values, SIDE, axis=-1)
    return jnp.where(coordinate == 0, edge_sign * rolled, rolled)


def lattice_shift(values, axis_dim, forward, edge_sign):
    extent = values.shape[axis_dim]
    position = lax.broadcasted_iota(jnp.int32, values.shape, axis_dim)
    if forward:
        rolled = jnp.roll(values, -1, axis=axis_dim)
        return jnp.where(position == extent - 1, edge_sign * rolled, rolled)
    rolled = jnp.roll(values, 1, axis=axis_dim)
    return jnp.where(position == 0, edge_sign * rolled, rolled)


def clover_apply(clover, spinor_pair):
    parts_real = []
    parts_imag = []
    for chiral in range(2):
        block_real = clover[chiral][:, :, :, 0::2, :]
        block_imag = clover[chiral][:, :, :, 1::2, :]
        total_real = 0.0
        total_imag = 0.0
        for column in range(6):
            spin_index = 2 * chiral + column // 3
            color_index = column % 3
            vector_real = spinor_pair[0][:, spin_index, :, :, color_index, :][:, None]
            vector_imag = spinor_pair[1][:, spin_index, :, :, color_index, :][:, None]
            entry_real = block_real[:, :, :, column, :]
            entry_imag = block_imag[:, :, :, column, :]
            total_real = total_real + entry_real * vector_real - entry_imag * vector_imag
            total_imag = total_imag + entry_real * vector_imag + entry_imag * vector_real
        counts = total_real.shape
        new_shape = (counts[0], 2, 3) + counts[2:]
        parts_real.append(total_real.reshape(new_shape).transpose(0, 1, 3, 4, 2, 5))
        parts_imag.append(total_imag.reshape(new_shape).transpose(0, 1, 3, 4, 2, 5))
    return (jnp.concatenate(parts_real, 1), jnp.concatenate(parts_imag, 1))


def recombine(direction, ahead_linked, behind_moved):
    top_part = pair_add(ahead_linked, behind_moved)
    bottom_part = pair_sub(spin_twist(direction, 1, behind_moved), spin_twist(direction, 1, ahead_linked))
    return (jnp.concatenate([top_part[0], bottom_part[0]], 1), jnp.concatenate([top_part[1], bottom_part[1]], 1))


def pair_map(function_one, value_pair):
    return (function_one(value_pair[0]), function_one(value_pair[1]))


def apply_operator(spinor_pair, gauge_links, clover, phase_signs):
    upper_half, lower_half = split_spins(spinor_pair)
    hopping = (0.0, 0.0)
    for direction in range(4):
        link_real = gauge_links[direction][:, :, :, 0::2, :]
        link_imag = gauge_links[direction][:, :, :, 1::2, :]
        twisted = spin_twist(direction, 0, lower_half)
        ahead_half = pair_sub(upper_half, twisted)
        behind_half = link_adjoint(link_real, link_imag, pair_add(upper_half, twisted))
        edge_sign = phase_signs[direction]
        if direction < 2:
            ahead_moved = pair_map(lambda values: plane_shift(values, direction, True, edge_sign), ahead_half)
            behind_moved = pair_map(lambda values: plane_shift(values, direction, False, edge_sign), behind_half)
        else:
            axis_dim = 3 if direction == 2 else 2
            ahead_moved = pair_map(lambda values: lattice_shift(values, axis_dim, True, edge_sign), ahead_half)
            behind_moved = pair_map(lambda values: lattice_shift(values, axis_dim, False, edge_sign), behind_half)
        ahead_linked = link_apply(link_real, link_imag, ahead_moved)
        hopping = pair_add(hopping, recombine(direction, ahead_linked, behind_moved))
    clovered = clover_apply(clover, spinor_pair)
    result = pair_add(pair_scale(diag_term, spinor_pair), clovered)
    return pair_sub(result, pair_scale(0.5, hopping))


def build_source(noise_field, dilution, time_index):
    sources = noise_field.shape[0]
    spin_mask = (lax.broadcasted_iota(jnp.int32, (sources, 4), 1) == lax.broadcasted_iota(jnp.int32, (sources, 4), 0) % 4).astype(jnp.float32)
    time_mask = (time_index[None, :] % DILUTE == dilution[:, None]).astype(jnp.float32)
    source_weight = spin_mask[:, :, None, None, None, None] * time_mask[:, None, :, None, None, None]
    return (source_weight * noise_field[:, None, :, :, 0::2, :], source_weight * noise_field[:, None, :, :, 1::2, :])


def project(solution, eigvecs):
    counts = solution[0].shape
    flat_shape = (counts[0] * counts[1], counts[2], counts[3] * counts[4] * counts[5])
    solve_result_real = solution[0].reshape(flat_shape)
    solve_result_imag = solution[1].reshape(flat_shape)
    eig_shape = (eigvecs.shape[0], eigvecs.shape[1], flat_shape[2])
    eigenmode_real = eigvecs[:, :, :, 0::2, :].reshape(eig_shape)
    eigenmode_imag = eigvecs[:, :, :, 1::2, :].reshape(eig_shape)
    highest_value = lax.Precision.HIGHEST
    real_component = jnp.einsum("gdc,xdc->xdg", eigenmode_real, solve_result_real, precision=highest_value) + jnp.einsum("gdc,xdc->xdg", eigenmode_imag, solve_result_imag, precision=highest_value)
    imaginary_component = jnp.einsum("gdc,xdc->xdg", eigenmode_real, solve_result_imag, precision=highest_value) - jnp.einsum("gdc,xdc->xdg", eigenmode_imag, solve_result_real, precision=highest_value)
    return jnp.concatenate([real_component, imaginary_component], 2)


def weigh_pairs(peram_block, partner):
    vectors = partner.shape[0]
    onehot = (partner[:, None] == lax.broadcasted_iota(jnp.int32, (vectors, vectors), 1)).astype(jnp.float32)
    highest_value = lax.Precision.HIGHEST
    real_component = jnp.einsum("jtk,kl->jtl", peram_block[:, :, :vectors], onehot, precision=highest_value)
    imaginary_component = jnp.einsum("jtk,kl->jtl", peram_block[:, :, vectors:], onehot, precision=highest_value)
    return jnp.concatenate([real_component, imaginary_component], 2)


def reference(noise_field, gauge_links, clover, eigvecs, partner, dilution, boundary):
    phase_signs = 1.0 - 2.0 * boundary.astype(jnp.float32)
    time_index = jnp.arange(NT, dtype=jnp.int32)
    source = build_source(noise_field, dilution, time_index)
    solution = pair_scale(step_size, source)
    for iteration in range(ITERS):
        applied = apply_operator(solution, gauge_links, clover, phase_signs)
        solution = pair_add(solution, pair_scale(step_size, pair_sub(source, applied)))
    perambulator = project(solution, eigvecs)
    weighted = weigh_pairs(perambulator, partner)
    correlator = jnp.einsum("jac,jbc->jab", weighted, perambulator, precision=lax.Precision.HIGHEST)
    return perambulator, correlator
```

```python
import jax
import jax.numpy as jnp
from jax import lax
from jax.experimental import pallas as pl
from jax.experimental.pallas import tpu as pltpu
from jax.sharding import PartitionSpec as P

ITERS = 4
DILUTE = 4
SIDE = 16
LANES = 128
diag_term = 4.1
step_size = 0.2
F32 = jnp.float32

twist_table = (
    (((1, 0, -1), (0, 0, -1)), ((1, 0, 1), (0, 0, 1))),
    (((1, -1, 0), (0, 1, 0)), ((1, 1, 0), (0, -1, 0))),
    (((0, 0, -1), (1, 0, 1)), ((0, 0, 1), (1, 0, -1))),
    (((0, 1, 0), (1, 1, 0)), ((0, 1, 0), (1, 1, 0))),
)


def add_scaled(pair, sign, coef, other):
    real_coef, imag_coef = coef
    if imag_coef == 0:
        if sign * real_coef > 0:
            return (pair[0] + other[0], pair[1] + other[1])
        return (pair[0] - other[0], pair[1] - other[1])
    if sign * imag_coef > 0:
        return (pair[0] - other[1], pair[1] + other[0])
    return (pair[0] + other[1], pair[1] - other[0])


def row8(ref, row):
    return ref[pl.ds(row, 8, stride=0), :]


def link_times(links, mu, half, vector, adjoint):
    out = []
    for i in range(3):
        real, imag = None, None
        for k in range(3):
            row, col = (k, i) if adjoint else (i, k)
            base = ((mu * 3 + row) * 6 + 2 * col) * 2 + half
            mr, mi = row8(links, base), row8(links, base + 2)
            vr, vi = vector[k]
            if adjoint:
                r, m = mr * vr + mi * vi, mr * vi - mi * vr
            else:
                r, m = mr * vr - mi * vi, mr * vi + mi * vr
            real = r if real is None else real + r
            imag = m if imag is None else imag + m
        out.append((real, imag))
    return out


def spinor_at(spin, color, part, half):
    return ((spin * 3 + color) * 2 + part) * 2 + half


def load_spin(ref, spin, half):
    return [
        tuple(ref[spinor_at(spin, c, p, half)] for p in range(2)) for c in range(3)
    ]


def store_spin(ref, spin, half, value):
    for c in range(3):
        for p in range(2):
            ref[spinor_at(spin, c, p, half)] = value[c][p]


def half_spin(mu, comp, sign, upper, lower):
    _, real_coef, imag_coef = twist_table[mu][0][comp]
    return [
        add_scaled(upper[c], sign, (real_coef, imag_coef), lower[c]) for c in range(3)
    ]


def lower_target(mu, comp):
    for target in range(2):
        source, real_coef, imag_coef = twist_table[mu][1][target]
        if source == comp:
            return target, (real_coef, imag_coef)
    raise ValueError


def lower_source(mu, comp):
    return twist_table[mu][0][comp][0]


def accumulate(top, bottom, mu, comp, sign, hopped):
    _, coef = lower_target(mu, comp)
    top = [(top[c][0] + hopped[c][0], top[c][1] + hopped[c][1]) for c in range(3)]
    bottom = [add_scaled(bottom[c], sign, coef, hopped[c]) for c in range(3)]
    return top, bottom


def source_rows(shape):
    return lax.broadcasted_iota(jnp.int32, shape, 0)


def spin_mask(spin):
    return source_rows((8, LANES)) % 4 == spin


def prepare_kernel(time_rank, space_rank, last_time, last_space, bounds, dilution, noise, links_in,
                   links, source, behind_time, behind_space):
    lane = lax.broadcasted_iota(jnp.int32, (8, LANES), 1)
    row = lax.broadcasted_iota(jnp.int32, (8, LANES), 0)
    phases = [(1 - 2 * bounds[mu]).astype(F32) * (0.5 * step_size) for mu in range(4)]
    plain = 0.5 * step_size
    at_x = jnp.where(lane % SIDE == SIDE - 1, phases[0], plain)
    at_y = jnp.where((lane >= LANES - SIDE) & (row % 2 == 1), phases[1], plain)
    at_z = jnp.full((8, LANES), jnp.where(space_rank[0] == last_space, phases[2], plain))
    at_t = jnp.full((8, LANES), jnp.where(time_rank[0] == last_time, phases[3], plain))
    scales = (at_x, at_y, at_z, at_t)
    for block in range(18):
        first, last = (block * 8) // 36, (block * 8 + 7) // 36
        scale = scales[first]
        if last != first:
            scale = jnp.where(row + block * 8 >= last * 36, scales[last], scale)
        links[block * 8 : block * 8 + 8, :] = links_in[block * 8 : block * 8 + 8, :] * scale
    weight = jnp.zeros((8, LANES), F32)
    for j in range(8):
        on = jnp.where(time_rank[0] % DILUTE == dilution[j], step_size, 0.0)
        weight = jnp.where(row == j, on, weight)
    for half in range(2):
        vector = []
        for c in range(3):
            pair = []
            for p in range(2):
                plane = (c * 2 + p) * 2 + half
                value = noise[pl.ds(plane, 8, stride=12), :] * weight
                source[plane] = value
                pair.append(value)
            vector.append(tuple(pair))
        for mu, out in ((3, behind_time), (2, behind_space)):
            moved = link_times(links, mu, half, vector, True)
            store_spin(out, 0, half, moved)


def shift_x(value, forward):
    lane = lax.broadcasted_iota(jnp.int32, (8, LANES), 1) % SIDE
    if forward:
        return jnp.where(
            lane == SIDE - 1,
            pltpu.roll(value, SIDE - 1, 1),
            pltpu.roll(value, LANES - 1, 1),
        )
    return jnp.where(
        lane == 0, pltpu.roll(value, LANES - SIDE + 1, 1), pltpu.roll(value, 1, 1)
    )


def shift_y(low, high, forward):
    lane = lax.broadcasted_iota(jnp.int32, (8, LANES), 1)
    if forward:
        a, b = pltpu.roll(low, LANES - SIDE, 1), pltpu.roll(high, LANES - SIDE, 1)
        keep = lane < LANES - SIDE
    else:
        a, b = pltpu.roll(low, SIDE, 1), pltpu.roll(high, SIDE, 1)
        keep = lane >= SIDE
    return jnp.where(keep, a, b), jnp.where(keep, b, a)


def shift_plane(mu, pair_of_halves, forward):
    moved = ([], [])
    for c in range(3):
        parts = ([], [])
        for p in range(2):
            low, high = pair_of_halves[0][c][p], pair_of_halves[1][c][p]
            if mu == 0:
                low, high = shift_x(low, forward), shift_x(high, forward)
            else:
                low, high = shift_y(low, high, forward)
            parts[0].append(low)
            parts[1].append(high)
        moved[0].append(tuple(parts[0]))
        moved[1].append(tuple(parts[1]))
    return moved


def local_body(load, links, clover, source, out):
    for chiral in range(2):
        for half in range(2):
            vector = load(2 * chiral, half) + load(2 * chiral + 1, half)
            for a in range(6):
                real, imag = None, None
                for b in range(6):
                    base = ((chiral * 6 + a) * 12 + 2 * b) * 2 + half
                    mr, mi = row8(clover, base), row8(clover, base + 2)
                    vr, vi = vector[b]
                    r, m = mr * vr - mi * vi, mr * vi + mi * vr
                    real = r if real is None else real + r
                    imag = m if imag is None else imag + m
                spin, color = 2 * chiral + a // 3, a % 3
                here = spin_mask(spin)
                keep = 1.0 - step_size * diag_term
                for p, total in ((0, real), (1, imag)):
                    value = keep * vector[a][p] - step_size * total
                    value = value + jnp.where(here, source[(color * 2 + p) * 2 + half], 0.0)
                    out[spinor_at(spin, color, p, half)] = value
    for comp in range(2):
        low_spin = 2 + lower_source(0, comp)
        upper = [load(comp, half) for half in range(2)]
        lower = [load(low_spin, half) for half in range(2)]
        top = [load_spin(out, comp, half) for half in range(2)]
        bottom = [load_spin(out, low_spin, half) for half in range(2)]
        for mu in range(2):
            ahead = [half_spin(mu, comp, -1, upper[h], lower[h]) for h in range(2)]
            ahead = shift_plane(mu, ahead, True)
            for h in range(2):
                hopped = link_times(links, mu, h, ahead[h], False)
                top[h], bottom[h] = accumulate(top[h], bottom[h], mu, comp, -1, hopped)
            behind = [
                link_times(links, mu, h, half_spin(mu, comp, 1, upper[h], lower[h]), True)
                for h in range(2)
            ]
            behind = shift_plane(mu, behind, False)
            for h in range(2):
                top[h], bottom[h] = accumulate(top[h], bottom[h], mu, comp, 1, behind[h])
        for h in range(2):
            store_spin(out, comp, h, top[h])
            store_spin(out, low_spin, h, bottom[h])


def source_spinor(source):
    def load(spin, half):
        here = spin_mask(spin)
        return [
            tuple(jnp.where(here, source[(c * 2 + p) * 2 + half], 0.0) for p in range(2))
            for c in range(3)
        ]

    return load


def local_first_kernel(links, clover, source, out):
    local_body(source_spinor(source), links, clover, source, out)


def local_kernel(solution, links, clover, source, out):
    local_body(lambda spin, half: load_spin(solution, spin, half), links, clover, source, out)


def hops(local, links, received, comp, half):
    top, bottom = load_spin(local, comp, half), load_spin(local, 2 + comp, half)
    for mu, ahead, behind in received:
        hopped = link_times(links, mu, half, ahead(comp, half, mu, -1), False)
        top, bottom = accumulate(top, bottom, mu, comp, -1, hopped)
        top, bottom = accumulate(top, bottom, mu, comp, 1, behind(comp, half, mu, 1))
    return top, bottom


def from_halves(ref):
    return lambda comp, half, mu, sign: load_spin(ref, comp, half)


def from_source(ref):
    def load(comp, half, mu, sign):
        whole = source_spinor(ref)
        return half_spin(mu, comp, sign, whole(comp, half), whole(2 + comp, half))

    return load


def step_body(kind, local, links, at, bt, az, bz, solution, sat, sbt, saz, sbz):
    received = ((3, kind(at), kind(bt)), (2, kind(az), kind(bz)))
    for comp in range(2):
        for half in range(2):
            top, bottom = hops(local, links, received, comp, half)
            store_spin(solution, comp, half, top)
            store_spin(solution, 2 + comp, half, bottom)
            for mu, ahead, behind in ((3, sat, sbt), (2, saz, sbz)):
                store_spin(ahead, comp, half, half_spin(mu, comp, -1, top, bottom))
                plus = half_spin(mu, comp, 1, top, bottom)
                store_spin(behind, comp, half, link_times(links, mu, half, plus, True))


def step_first_kernel(*refs):
    step_body(from_source, *refs)


def step_kernel(*refs):
    step_body(from_halves, *refs)


def modes_kernel(modes, out):
    count = modes.shape[0] // 12
    out[...] = jnp.zeros(out.shape, out.dtype)
    for c in range(3):
        for half in range(2):
            real = modes[pl.ds(4 * c + half, count, stride=12), :]
            imag = modes[pl.ds(4 * c + 2 + half, count, stride=12), :]
            lanes = slice(half * LANES, half * LANES + LANES)
            for p, upper, lower in ((0, real, -imag), (1, imag, real)):
                for start, value in ((0, upper), (count, lower)):
                    high = value.astype(jnp.bfloat16)
                    low = (value - high.astype(F32)).astype(jnp.bfloat16)
                    out[2 * c + p, start : start + count, lanes] = high
                    out[2 * c + p, 128 + start : 128 + start + count, lanes] = low


def last_kernel(local, links, at, bt, az, bz, modes, out, rows):
    received = (
        (3, from_halves(at), from_halves(bt)),
        (2, from_halves(az), from_halves(bz)),
    )
    for comp in range(2):
        for half in range(2):
            pair = hops(local, links, received, comp, half)
            for spin, value in zip((comp, 2 + comp), pair, strict=True):
                for c in range(3):
                    for p in range(2):
                        rows[2 * c + p, 8 * spin : 8 * spin + 8, half * LANES : half * LANES + LANES] = value[c][p]
    total = None
    for plane in range(6):
        value = rows[plane]
        high = value.astype(jnp.bfloat16)
        low = (value - high.astype(F32)).astype(jnp.bfloat16)
        product = lax.dot_general(
            jnp.concatenate([high, low], 0),
            modes[plane],
            (((1,), (1,)), ((), ())),
            preferred_element_type=F32,
        )
        total = product if total is None else total + product
    total = total[:32, :128] + (total[:32, 128:] + total[32:, :128])
    for spin in range(4):
        out[pl.ds(spin, 8, stride=4), :] = total[8 * spin : 8 * spin + 8, : out.shape[1]]


def sum_kernel(parts, out):
    out[...] = jnp.sum(parts[...], axis=0, keepdims=True)


def correlate_kernel(row, rows, partner, out):
    size = row.shape[1]
    onehot = (
        partner[...] == lax.broadcasted_iota(jnp.int32, (size, size), 0)
    ).astype(F32)
    contract = (((1,), (1,)), ((), ()))
    own = jnp.broadcast_to(row[...], (8, size))
    weighted = lax.dot_general(
        own, onehot, contract, precision=lax.Precision.HIGHEST, preferred_element_type=F32
    )
    found = lax.dot_general(
        weighted, rows[...], contract, precision=lax.Precision.HIGHEST, preferred_element_type=F32
    )
    out[...] = found[:1]


def call(kernel, outs, flops, scalars, *args, scratch=()):
    vmem = pl.BlockSpec(memory_space=pltpu.VMEM)
    smem = pl.BlockSpec(memory_space=pltpu.SMEM)
    single = not isinstance(outs, (list, tuple))
    shapes = [outs] if single else list(outs)
    moved = 4 * sum(a.size for a in args) + 4 * sum(s.size for s in shapes)
    out = pl.pallas_call(
        kernel,
        out_shape=outs,
        in_specs=[smem] * len(scalars) + [vmem] * len(args),
        out_specs=vmem if single else [vmem] * len(shapes),
        scratch_shapes=scratch,
        compiler_params=pltpu.CompilerParams(vmem_limit_bytes=16 << 20),
        cost_estimate=pl.CostEstimate(flops=flops, bytes_accessed=moved, transcendentals=0),
    )(*scalars, *args)
    return out


def vectors(count):
    return jax.ShapeDtypeStruct((count, 8, LANES), F32)


def exchange(ahead_time, behind_time, ahead_space, behind_space):
    def ring(axis, step):
        size = lax.axis_size(axis)
        return [(i, (i + step) % size) for i in range(size)]

    az = lax.ppermute(ahead_space, "space", ring("space", -1))
    bz = lax.ppermute(behind_space, "space", ring("space", 1))
    at = lax.ppermute(ahead_time, "tm", ring("tm", -1))
    bt = lax.ppermute(behind_time, "tm", ring("tm", 1))
    return at, bt, az, bz


def partial_rows(noise_field, gauge_links, clover, eigvecs, dilution, boundary):
    count = eigvecs.shape[0]
    noise = noise_field.reshape(-1, LANES)
    links_in = gauge_links.reshape(-1, LANES)
    clover = clover.reshape(-1, LANES)
    modes_in = eigvecs.reshape(-1, LANES)
    time_rank = lax.axis_index("tm").astype(jnp.int32).reshape(1)
    space_rank = lax.axis_index("space").astype(jnp.int32).reshape(1)
    last_time, last_space = lax.axis_size("tm") - 1, lax.axis_size("space") - 1

    def prepare(tr, sr, *refs):
        prepare_kernel(tr, sr, last_time, last_space, *refs)

    links, source, behind_time, behind_space = call(
        prepare,
        [jax.ShapeDtypeStruct(links_in.shape, F32), vectors(12), vectors(12), vectors(12)],
        10**6,
        (time_rank, space_rank, boundary, dilution),
        noise,
        links_in,
    )
    sends = (source, behind_time, source, behind_space)
    solution = None
    for iteration in range(ITERS):
        at, bt, az, bz = exchange(*sends)
        if iteration == 0:
            local = call(local_first_kernel, vectors(48), 5 * 10**6, (), links, clover, source)
            modes = call(
                modes_kernel,
                jax.ShapeDtypeStruct((6, 256, 256), jnp.bfloat16),
                10**6,
                (),
                modes_in,
            )
        else:
            local = call(local_kernel, vectors(48), 5 * 10**6, (), solution, links, clover, source)
        if iteration < ITERS - 1:
            body = step_first_kernel if iteration == 0 else step_kernel
            solution, *sends = call(
                body,
                [vectors(48)] + [vectors(24)] * 4,
                3 * 10**6,
                (),
                local, links, at, bt, az, bz,
            )
        else:
            partial_sums = call(
                last_kernel,
                jax.ShapeDtypeStruct((32, 2 * count), F32),
                10**7,
                (),
                local, links, at, bt, az, bz, modes,
                scratch=[pltpu.VMEM((6, 32, 256), F32)],
            )
    return partial_sums


def shards(noise_field, gauge_links, clover, eigvecs, partner, dilution, boundary):
    count = eigvecs.shape[0]
    partial_sums = partial_rows(
        noise_field, gauge_links, clover, eigvecs, dilution, boundary
    )
    parts = lax.all_to_all(partial_sums, "space", 0, 0, tiled=True)
    row = call(sum_kernel, jax.ShapeDtypeStruct((1, 2 * count), F32), 10**4, (), parts)
    times = lax.axis_size("tm")
    rows = lax.all_to_all(jnp.broadcast_to(row, (times, 2 * count)), "tm", 0, 0, tiled=True)
    both = jnp.concatenate([partner, partner + count]).reshape(1, 2 * count)
    correlator = call(
        correlate_kernel, jax.ShapeDtypeStruct((1, times), F32), 10**5, (), row, rows, both
    )
    return row.reshape(1, 1, 2 * count), correlator.reshape(1, 1, times)


def solution(mesh):
    return jax.shard_map(
        shards,
        mesh=mesh,
        in_specs=(
            P(None, "tm", "space", None, None),
            P(None, None, "tm", "space", None, None),
            P(None, None, "tm", "space", None, None),
            P(None, "tm", "space", None, None),
            P(),
            P(),
            P(),
        ),
        out_specs=(P("space", "tm", None), P("space", "tm", None)),
        check_vma=False,
    )
```

```python
import jax
import jax.numpy as jnp
from jax import lax
from jax.experimental import pallas as pl
from jax.experimental.pallas import tpu as pltpu
from jax.sharding import PartitionSpec as P

ITERS = 4
DILUTE = 4
SIDE = 16
LANES = 128
diag_term = 4.1
step_size = 0.2
F32 = jnp.float32

twist_table = (
    (((1, 0, -1), (0, 0, -1)), ((1, 0, 1), (0, 0, 1))),
    (((1, -1, 0), (0, 1, 0)), ((1, 1, 0), (0, -1, 0))),
    (((0, 0, -1), (1, 0, 1)), ((0, 0, 1), (1, 0, -1))),
    (((0, 1, 0), (1, 1, 0)), ((0, 1, 0), (1, 1, 0))),
)


def add_scaled(pair, sign, coef, other):
    real_coef, imag_coef = coef
    if imag_coef == 0:
        if sign * real_coef > 0:
            return (pair[0] + other[0], pair[1] + other[1])
        return (pair[0] - other[0], pair[1] - other[1])
    if sign * imag_coef > 0:
        return (pair[0] - other[1], pair[1] + other[0])
    return (pair[0] + other[1], pair[1] - other[0])


def row8(ref, row):
    return ref[pl.ds(row, 8, stride=0), :]


def link_times(links, mu, half, vector, adjoint):
    out = []
    for i in range(3):
        real, imag = None, None
        for k in range(3):
            row, col = (k, i) if adjoint else (i, k)
            base = ((mu * 3 + row) * 6 + 2 * col) * 2 + half
            mr, mi = row8(links, base), row8(links, base + 2)
            vr, vi = vector[k]
            if adjoint:
                r, m = mr * vr + mi * vi, mr * vi - mi * vr
            else:
                r, m = mr * vr - mi * vi, mr * vi + mi * vr
            real = r if real is None else real + r
            imag = m if imag is None else imag + m
        out.append((real, imag))
    return out


def spinor_at(spin, color, part, half):
    return ((spin * 3 + color) * 2 + part) * 2 + half


def load_spin(ref, spin, half):
    return [
        tuple(ref[spinor_at(spin, c, p, half)] for p in range(2)) for c in range(3)
    ]


def store_spin(ref, spin, half, value):
    for c in range(3):
        for p in range(2):
            ref[spinor_at(spin, c, p, half)] = value[c][p]


def half_spin(mu, comp, sign, upper, lower):
    _, real_coef, imag_coef = twist_table[mu][0][comp]
    return [
        add_scaled(upper[c], sign, (real_coef, imag_coef), lower[c]) for c in range(3)
    ]


def lower_target(mu, comp):
    for target in range(2):
        source, real_coef, imag_coef = twist_table[mu][1][target]
        if source == comp:
            return target, (real_coef, imag_coef)
    raise ValueError


def lower_source(mu, comp):
    return twist_table[mu][0][comp][0]


def accumulate(top, bottom, mu, comp, sign, hopped):
    _, coef = lower_target(mu, comp)
    top = [(top[c][0] + hopped[c][0], top[c][1] + hopped[c][1]) for c in range(3)]
    bottom = [add_scaled(bottom[c], sign, coef, hopped[c]) for c in range(3)]
    return top, bottom


def source_rows(shape):
    return lax.broadcasted_iota(jnp.int32, shape, 0)


def spin_mask(spin):
    return source_rows((8, LANES)) % 4 == spin


class Pick:
    def __init__(self, first, here, there):
        self.first, self.here, self.there = first, here, there

    def __getitem__(self, index):
        return jnp.where(self.first, self.here[index], self.there[index])


def is_even(rank):
    return jnp.full((8, LANES), rank[0], jnp.int32) % 2 == 0


def store_sends(inner, outer, even, comp, half, behind, ahead):
    for c in range(3):
        for p in range(2):
            up, down = behind[c][p], ahead[c][p]
            inner[spinor_at(comp, c, p, half)] = jnp.where(even, up, down)
            outer[spinor_at(comp, c, p, half)] = jnp.where(even, down, up)


def prepare_kernel(last_time, last_space, time_rank, space_rank, bits, noise, links_in,
                   links, source, t_inner, t_outer, z_inner, z_outer):
    lane = lax.broadcasted_iota(jnp.int32, (8, LANES), 1)
    row = lax.broadcasted_iota(jnp.int32, (8, LANES), 0)
    phases = [(1 - 2 * bits[mu]).astype(F32) * (0.5 * step_size) for mu in range(4)]
    plain = 0.5 * step_size
    at_x = jnp.where(lane % SIDE == SIDE - 1, phases[0], plain)
    at_y = jnp.where((lane >= LANES - SIDE) & (row % 2 == 1), phases[1], plain)
    at_z = jnp.full((8, LANES), jnp.where(space_rank[0] == last_space, phases[2], plain))
    at_t = jnp.full((8, LANES), jnp.where(time_rank[0] == last_time, phases[3], plain))
    scales = (at_x, at_y, at_z, at_t)
    for block in range(18):
        first, last = (block * 8) // 36, (block * 8 + 7) // 36
        scale = scales[first]
        if last != first:
            scale = jnp.where(row + block * 8 >= last * 36, scales[last], scale)
        links[block * 8 : block * 8 + 8, :] = links_in[block * 8 : block * 8 + 8, :] * scale
    weight = jnp.zeros((8, LANES), F32)
    for j in range(8):
        on = jnp.where(time_rank[0] % DILUTE == bits[4 + j], step_size, 0.0)
        weight = jnp.where(row == j, on, weight)
    for half in range(2):
        vector = []
        for c in range(3):
            pair = []
            for p in range(2):
                plane = (c * 2 + p) * 2 + half
                value = noise[pl.ds(plane, 8, stride=12), :] * weight
                source[plane] = value
                pair.append(value)
            vector.append(tuple(pair))
        for mu, rank, inner, outer in (
            (3, time_rank, t_inner, t_outer),
            (2, space_rank, z_inner, z_outer),
        ):
            moved = link_times(links, mu, half, vector, True)
            store_sends(inner, outer, is_even(rank), 0, half, moved, vector)


def shift_x(value, forward):
    lane = lax.broadcasted_iota(jnp.int32, (8, LANES), 1) % SIDE
    if forward:
        return jnp.where(
            lane == SIDE - 1,
            pltpu.roll(value, SIDE - 1, 1),
            pltpu.roll(value, LANES - 1, 1),
        )
    return jnp.where(
        lane == 0, pltpu.roll(value, LANES - SIDE + 1, 1), pltpu.roll(value, 1, 1)
    )


def shift_y(low, high, forward):
    lane = lax.broadcasted_iota(jnp.int32, (8, LANES), 1)
    if forward:
        a, b = pltpu.roll(low, LANES - SIDE, 1), pltpu.roll(high, LANES - SIDE, 1)
        keep = lane < LANES - SIDE
    else:
        a, b = pltpu.roll(low, SIDE, 1), pltpu.roll(high, SIDE, 1)
        keep = lane >= SIDE
    return jnp.where(keep, a, b), jnp.where(keep, b, a)


def shift_plane(mu, pair_of_halves, forward):
    moved = ([], [])
    for c in range(3):
        parts = ([], [])
        for p in range(2):
            low, high = pair_of_halves[0][c][p], pair_of_halves[1][c][p]
            if mu == 0:
                low, high = shift_x(low, forward), shift_x(high, forward)
            else:
                low, high = shift_y(low, high, forward)
            parts[0].append(low)
            parts[1].append(high)
        moved[0].append(tuple(parts[0]))
        moved[1].append(tuple(parts[1]))
    return moved


def local_body(load, links, clover, source, out):
    for chiral in range(2):
        for half in range(2):
            vector = load(2 * chiral, half) + load(2 * chiral + 1, half)
            for a in range(6):
                real, imag = None, None
                for b in range(6):
                    base = ((chiral * 6 + a) * 12 + 2 * b) * 2 + half
                    mr, mi = row8(clover, base), row8(clover, base + 2)
                    vr, vi = vector[b]
                    r, m = mr * vr - mi * vi, mr * vi + mi * vr
                    real = r if real is None else real + r
                    imag = m if imag is None else imag + m
                spin, color = 2 * chiral + a // 3, a % 3
                here = spin_mask(spin)
                keep = 1.0 - step_size * diag_term
                for p, total in ((0, real), (1, imag)):
                    value = keep * vector[a][p] - step_size * total
                    value = value + jnp.where(here, source[(color * 2 + p) * 2 + half], 0.0)
                    out[spinor_at(spin, color, p, half)] = value
    for comp in range(2):
        low_spin = 2 + lower_source(0, comp)
        upper = [load(comp, half) for half in range(2)]
        lower = [load(low_spin, half) for half in range(2)]
        top = [load_spin(out, comp, half) for half in range(2)]
        bottom = [load_spin(out, low_spin, half) for half in range(2)]
        for mu in range(2):
            ahead = [half_spin(mu, comp, -1, upper[h], lower[h]) for h in range(2)]
            ahead = shift_plane(mu, ahead, True)
            for h in range(2):
                hopped = link_times(links, mu, h, ahead[h], False)
                top[h], bottom[h] = accumulate(top[h], bottom[h], mu, comp, -1, hopped)
            behind = [
                link_times(links, mu, h, half_spin(mu, comp, 1, upper[h], lower[h]), True)
                for h in range(2)
            ]
            behind = shift_plane(mu, behind, False)
            for h in range(2):
                top[h], bottom[h] = accumulate(top[h], bottom[h], mu, comp, 1, behind[h])
        for h in range(2):
            store_spin(out, comp, h, top[h])
            store_spin(out, low_spin, h, bottom[h])


def source_spinor(source):
    def load(spin, half):
        here = spin_mask(spin)
        return [
            tuple(jnp.where(here, source[(c * 2 + p) * 2 + half], 0.0) for p in range(2))
            for c in range(3)
        ]

    return load


def local_first_kernel(links, clover, source, out):
    local_body(source_spinor(source), links, clover, source, out)


def local_kernel(solution, links, clover, source, out):
    local_body(lambda spin, half: load_spin(solution, spin, half), links, clover, source, out)


def hops(local, links, received, comp, half):
    top, bottom = load_spin(local, comp, half), load_spin(local, 2 + comp, half)
    for mu, ahead, behind in received:
        hopped = link_times(links, mu, half, ahead(comp, half, mu, -1), False)
        top, bottom = accumulate(top, bottom, mu, comp, -1, hopped)
        top, bottom = accumulate(top, bottom, mu, comp, 1, behind(comp, half, mu, 1))
    return top, bottom


def from_halves(ref):
    return lambda comp, half, mu, sign: load_spin(ref, comp, half)


def from_source(ref):
    def load(comp, half, mu, sign):
        whole = source_spinor(ref)
        return half_spin(mu, comp, sign, whole(comp, half), whole(2 + comp, half))

    return load


def arrivals(kind, time_rank, space_rank, t_inner, t_outer, z_inner, z_outer):
    received = []
    for mu, rank, inner, outer in (
        (3, time_rank, t_inner, t_outer),
        (2, space_rank, z_inner, z_outer),
    ):
        even = is_even(rank)
        received.append((mu, kind(Pick(even, inner, outer)), kind(Pick(even, outer, inner))))
    return received


def step_body(kind, time_rank, space_rank, local, links, ti, to, zi, zo, solution, *sends):
    received = arrivals(kind, time_rank, space_rank, ti, to, zi, zo)
    for comp in range(2):
        for half in range(2):
            top, bottom = hops(local, links, received, comp, half)
            store_spin(solution, comp, half, top)
            store_spin(solution, 2 + comp, half, bottom)
            for mu, rank, inner, outer in (
                (3, time_rank, *sends[:2]),
                (2, space_rank, *sends[2:]),
            ):
                ahead = half_spin(mu, comp, -1, top, bottom)
                plus = half_spin(mu, comp, 1, top, bottom)
                behind = link_times(links, mu, half, plus, True)
                store_sends(inner, outer, is_even(rank), comp, half, behind, ahead)


def step_first_kernel(*refs):
    step_body(from_source, *refs)


def step_kernel(*refs):
    step_body(from_halves, *refs)


def modes_kernel(modes, out):
    count = modes.shape[0] // 12
    out[...] = jnp.zeros(out.shape, out.dtype)
    for c in range(3):
        for half in range(2):
            real = modes[pl.ds(4 * c + half, count, stride=12), :]
            imag = modes[pl.ds(4 * c + 2 + half, count, stride=12), :]
            lanes = slice(half * LANES, half * LANES + LANES)
            for p, upper, lower in ((0, real, -imag), (1, imag, real)):
                for start, value in ((0, upper), (count, lower)):
                    high = value.astype(jnp.bfloat16)
                    low = (value - high.astype(F32)).astype(jnp.bfloat16)
                    out[2 * c + p, start : start + count, lanes] = high
                    out[2 * c + p, 128 + start : 128 + start + count, lanes] = low


def last_kernel(time_rank, space_rank, local, links, ti, to, zi, zo, modes, out, rows):
    received = arrivals(from_halves, time_rank, space_rank, ti, to, zi, zo)
    for comp in range(2):
        for half in range(2):
            pair = hops(local, links, received, comp, half)
            for spin, value in zip((comp, 2 + comp), pair, strict=True):
                for c in range(3):
                    for p in range(2):
                        rows[2 * c + p, 8 * spin : 8 * spin + 8, half * LANES : half * LANES + LANES] = value[c][p]
    total = None
    for plane in range(6):
        value = rows[plane]
        high = value.astype(jnp.bfloat16)
        low = (value - high.astype(F32)).astype(jnp.bfloat16)
        product = lax.dot_general(
            jnp.concatenate([high, low], 0),
            modes[plane],
            (((1,), (1,)), ((), ())),
            preferred_element_type=F32,
        )
        total = product if total is None else total + product
    total = total[:32, :128] + (total[:32, 128:] + total[32:, :128])
    for spin in range(4):
        out[pl.ds(spin, 8, stride=4), :] = total[8 * spin : 8 * spin + 8, : out.shape[1]]


def sum_kernel(parts, out, copies):
    total = jnp.sum(parts[...], axis=0, keepdims=True)
    out[...] = total
    copies[...] = jnp.broadcast_to(total, copies.shape)


def correlate_kernel(row, rows, partner, out):
    size = row.shape[1]
    onehot = (
        partner[...] == lax.broadcasted_iota(jnp.int32, (size, size), 0)
    ).astype(F32)
    contract = (((1,), (1,)), ((), ()))
    own = jnp.broadcast_to(row[...], (8, size))
    weighted = lax.dot_general(
        own, onehot, contract, precision=lax.Precision.HIGHEST, preferred_element_type=F32
    )
    found = lax.dot_general(
        weighted, rows[...], contract, precision=lax.Precision.HIGHEST, preferred_element_type=F32
    )
    out[...] = found[:1]


def call(kernel, outs, flops, scalars, *args, scratch=()):
    vmem = pl.BlockSpec(memory_space=pltpu.VMEM)
    smem = pl.BlockSpec(memory_space=pltpu.SMEM)
    single = not isinstance(outs, (list, tuple))
    shapes = [outs] if single else list(outs)
    moved = 4 * sum(a.size for a in args) + 4 * sum(s.size for s in shapes)
    out = pl.pallas_call(
        kernel,
        out_shape=outs,
        in_specs=[smem] * len(scalars) + [vmem] * len(args),
        out_specs=vmem if single else [vmem] * len(shapes),
        scratch_shapes=scratch,
        compiler_params=pltpu.CompilerParams(vmem_limit_bytes=16 << 20),
        cost_estimate=pl.CostEstimate(flops=flops, bytes_accessed=moved, transcendentals=0),
    )(*scalars, *args)
    return out


def vectors(count):
    return jax.ShapeDtypeStruct((count, 8, LANES), F32)


def exchange(t_inner, t_outer, z_inner, z_outer):
    def swap(axis, shift):
        size = lax.axis_size(axis)
        pairs = [((i + shift) % size, (i + 1 + shift) % size) for i in range(0, size, 2)]
        return pairs + [(j, i) for i, j in pairs]

    zi = lax.ppermute(z_inner, "space", swap("space", 0))
    zo = lax.ppermute(z_outer, "space", swap("space", 1))
    ti = lax.ppermute(t_inner, "tm", swap("tm", 0))
    to = lax.ppermute(t_outer, "tm", swap("tm", 1))
    return ti, to, zi, zo


def partial_rows(noise_field, gauge_links, clover, eigvecs, dilution, boundary):
    count = eigvecs.shape[0]
    noise = noise_field.reshape(-1, LANES)
    links_in = gauge_links.reshape(-1, LANES)
    clover = clover.reshape(-1, LANES)
    modes_in = eigvecs.reshape(-1, LANES)
    time_rank = lax.axis_index("tm").astype(jnp.int32).reshape(1)
    space_rank = lax.axis_index("space").astype(jnp.int32).reshape(1)
    last_time, last_space = lax.axis_size("tm") - 1, lax.axis_size("space") - 1

    ranks = (time_rank, space_rank)

    def prepare(*refs):
        prepare_kernel(last_time, last_space, *refs)

    links, source, *sends = call(
        prepare,
        [jax.ShapeDtypeStruct(links_in.shape, F32)] + [vectors(12)] * 5,
        10**6,
        (*ranks, jnp.concatenate([boundary, dilution])),
        noise,
        links_in,
    )
    solution = None
    for iteration in range(ITERS):
        arrived = exchange(*sends)
        if iteration == 0:
            local = call(local_first_kernel, vectors(48), 5 * 10**6, (), links, clover, source)
            modes = call(
                modes_kernel,
                jax.ShapeDtypeStruct((6, 256, 256), jnp.bfloat16),
                10**6,
                (),
                modes_in,
            )
        else:
            local = call(local_kernel, vectors(48), 5 * 10**6, (), solution, links, clover, source)
        if iteration < ITERS - 1:
            body = step_first_kernel if iteration == 0 else step_kernel
            solution, *sends = call(
                body,
                [vectors(48)] + [vectors(24)] * 4,
                3 * 10**6,
                ranks,
                local, links, *arrived,
            )
        else:
            partial_sums = call(
                last_kernel,
                jax.ShapeDtypeStruct((32, 2 * count), F32),
                10**7,
                ranks,
                local, links, *arrived, modes,
                scratch=[pltpu.VMEM((6, 32, 256), F32)],
            )
    return partial_sums


def shards(noise_field, gauge_links, clover, eigvecs, partner, dilution, boundary):
    count = eigvecs.shape[0]
    partial_sums = partial_rows(
        noise_field, gauge_links, clover, eigvecs, dilution, boundary
    )
    parts = lax.all_to_all(partial_sums, "space", 0, 0, tiled=True)
    times = lax.axis_size("tm")
    row, copies = call(
        sum_kernel,
        [jax.ShapeDtypeStruct((n, 2 * count), F32) for n in (1, times)],
        10**4,
        (),
        parts,
    )
    rows = lax.all_to_all(copies, "tm", 0, 0, tiled=True)
    both = jnp.concatenate([partner, partner + count]).reshape(1, 2 * count)
    correlator = call(
        correlate_kernel, jax.ShapeDtypeStruct((1, times), F32), 10**5, (), row, rows, both
    )
    return row.reshape(1, 1, 2 * count), correlator.reshape(1, 1, times)


def solution(mesh):
    return jax.shard_map(
        shards,
        mesh=mesh,
        in_specs=(
            P(None, "tm", "space", None, None),
            P(None, None, "tm", "space", None, None),
            P(None, None, "tm", "space", None, None),
            P(None, "tm", "space", None, None),
            P(),
            P(),
            P(),
        ),
        out_specs=(P("space", "tm", None), P("space", "tm", None)),
        check_vma=False,
    )
```

```python
import jax
import jax.numpy as jnp
from jax import lax
from jax.experimental import pallas as pl
from jax.experimental.pallas import tpu as pltpu
from jax.sharding import PartitionSpec as P

ITERS = 4
DILUTE = 4
SIDE = 16
LANES = 128
diag_term = 4.1
step_size = 0.2
F32 = jnp.float32

twist_table = (
    (((1, 0, -1), (0, 0, -1)), ((1, 0, 1), (0, 0, 1))),
    (((1, -1, 0), (0, 1, 0)), ((1, 1, 0), (0, -1, 0))),
    (((0, 0, -1), (1, 0, 1)), ((0, 0, 1), (1, 0, -1))),
    (((0, 1, 0), (1, 1, 0)), ((0, 1, 0), (1, 1, 0))),
)


def add_scaled(pair, sign, coef, other):
    real_coef, imag_coef = coef
    if imag_coef == 0:
        if sign * real_coef > 0:
            return (pair[0] + other[0], pair[1] + other[1])
        return (pair[0] - other[0], pair[1] - other[1])
    if sign * imag_coef > 0:
        return (pair[0] - other[1], pair[1] + other[0])
    return (pair[0] + other[1], pair[1] - other[0])


def row8(ref, row):
    if isinstance(ref, PackedLinks):
        return jnp.where(ref.first, row8(ref.here, row + ref.shift), row8(ref.there, row + ref.shift))
    return ref[pl.ds(row, 8, stride=0), :]


class PackedLinks:
    def __init__(self, first, here, there, shift):
        self.first, self.here, self.there, self.shift = first, here, there, shift


def link_times(links, mu, half, vector, adjoint):
    out = []
    for i in range(3):
        real, imag = None, None
        for k in range(3):
            row, col = (k, i) if adjoint else (i, k)
            base = ((mu * 3 + row) * 6 + 2 * col) * 2 + half
            mr, mi = row8(links, base), row8(links, base + 2)
            vr, vi = vector[k]
            if adjoint:
                r, m = mr * vr + mi * vi, mr * vi - mi * vr
            else:
                r, m = mr * vr - mi * vi, mr * vi + mi * vr
            real = r if real is None else real + r
            imag = m if imag is None else imag + m
        out.append((real, imag))
    return out


def spinor_at(spin, color, part, half):
    return ((spin * 3 + color) * 2 + part) * 2 + half


def load_spin(ref, spin, half):
    return [
        tuple(ref[spinor_at(spin, c, p, half)] for p in range(2)) for c in range(3)
    ]


def store_spin(ref, spin, half, value):
    for c in range(3):
        for p in range(2):
            ref[spinor_at(spin, c, p, half)] = value[c][p]


def half_spin(mu, comp, sign, upper, lower):
    _, real_coef, imag_coef = twist_table[mu][0][comp]
    return [
        add_scaled(upper[c], sign, (real_coef, imag_coef), lower[c]) for c in range(3)
    ]


def lower_target(mu, comp):
    for target in range(2):
        source, real_coef, imag_coef = twist_table[mu][1][target]
        if source == comp:
            return target, (real_coef, imag_coef)
    raise ValueError


def lower_source(mu, comp):
    return twist_table[mu][0][comp][0]


def accumulate(top, bottom, mu, comp, sign, hopped):
    _, coef = lower_target(mu, comp)
    top = [(top[c][0] + hopped[c][0], top[c][1] + hopped[c][1]) for c in range(3)]
    bottom = [add_scaled(bottom[c], sign, coef, hopped[c]) for c in range(3)]
    return top, bottom


def source_rows(shape):
    return lax.broadcasted_iota(jnp.int32, shape, 0)


def spin_mask(spin):
    return source_rows((8, LANES)) % 4 == spin


class Pick:
    def __init__(self, first, here, there):
        self.first, self.here, self.there = first, here, there

    def __getitem__(self, index):
        return jnp.where(self.first, self.here[index], self.there[index])


def is_even(rank):
    return jnp.full((8, LANES), rank[0], jnp.int32) % 2 == 0


def store_sends(inner, outer, even, comp, half, behind, ahead):
    for c in range(3):
        for p in range(2):
            up, down = behind[c][p], ahead[c][p]
            inner[spinor_at(comp, c, p, half)] = jnp.where(even, up, down)
            outer[spinor_at(comp, c, p, half)] = jnp.where(even, down, up)


def source_weight(bits, time):
    row = source_rows((8, LANES))
    weight = jnp.zeros((8, LANES), F32)
    for j in range(8):
        on = jnp.where(time % DILUTE == bits[4 + j], step_size, 0.0)
        weight = jnp.where(row == j, on, weight)
    return weight


def hop_factor(bits, mu, crosses):
    phase = (1 - 2 * bits[mu]).astype(F32) * (0.5 * step_size)
    return jnp.where(crosses, phase, 0.5 * step_size)


def prepare_kernel(sizes, time_rank, space_rank, bits, noise, links_in, links, source):
    lane = lax.broadcasted_iota(jnp.int32, (8, LANES), 1)
    row = lax.broadcasted_iota(jnp.int32, (8, LANES), 0)
    at_x = hop_factor(bits, 0, lane % SIDE == SIDE - 1)
    at_y = hop_factor(bits, 1, (lane >= LANES - SIDE) & (row % 2 == 1))
    at_z = jnp.full((8, LANES), hop_factor(bits, 2, space_rank[0] == sizes[1] - 1))
    at_t = jnp.full((8, LANES), hop_factor(bits, 3, time_rank[0] == sizes[0] - 1))
    scales = (at_x, at_y, at_z, at_t)
    for block in range(18):
        first, last = (block * 8) // 36, (block * 8 + 7) // 36
        scale = scales[first]
        if last != first:
            scale = jnp.where(row + block * 8 >= last * 36, scales[last], scale)
        links[block * 8 : block * 8 + 8, :] = links_in[block * 8 : block * 8 + 8, :] * scale
    weight = source_weight(bits, time_rank[0])
    for plane in range(12):
        source[plane] = noise[pl.ds(plane, 8, stride=12), :] * weight


def shift_x(value, forward):
    lane = lax.broadcasted_iota(jnp.int32, (8, LANES), 1) % SIDE
    if forward:
        return jnp.where(
            lane == SIDE - 1,
            pltpu.roll(value, SIDE - 1, 1),
            pltpu.roll(value, LANES - 1, 1),
        )
    return jnp.where(
        lane == 0, pltpu.roll(value, LANES - SIDE + 1, 1), pltpu.roll(value, 1, 1)
    )


def shift_y(low, high, forward):
    lane = lax.broadcasted_iota(jnp.int32, (8, LANES), 1)
    if forward:
        a, b = pltpu.roll(low, LANES - SIDE, 1), pltpu.roll(high, LANES - SIDE, 1)
        keep = lane < LANES - SIDE
    else:
        a, b = pltpu.roll(low, SIDE, 1), pltpu.roll(high, SIDE, 1)
        keep = lane >= SIDE
    return jnp.where(keep, a, b), jnp.where(keep, b, a)


def shift_plane(mu, pair_of_halves, forward):
    moved = ([], [])
    for c in range(3):
        parts = ([], [])
        for p in range(2):
            low, high = pair_of_halves[0][c][p], pair_of_halves[1][c][p]
            if mu == 0:
                low, high = shift_x(low, forward), shift_x(high, forward)
            else:
                low, high = shift_y(low, high, forward)
            parts[0].append(low)
            parts[1].append(high)
        moved[0].append(tuple(parts[0]))
        moved[1].append(tuple(parts[1]))
    return moved


def local_body(load, links, clover, source, out):
    for chiral in range(2):
        for half in range(2):
            vector = load(2 * chiral, half) + load(2 * chiral + 1, half)
            for a in range(6):
                real, imag = None, None
                for b in range(6):
                    base = ((chiral * 6 + a) * 12 + 2 * b) * 2 + half
                    mr, mi = row8(clover, base), row8(clover, base + 2)
                    vr, vi = vector[b]
                    r, m = mr * vr - mi * vi, mr * vi + mi * vr
                    real = r if real is None else real + r
                    imag = m if imag is None else imag + m
                spin, color = 2 * chiral + a // 3, a % 3
                here = spin_mask(spin)
                keep = 1.0 - step_size * diag_term
                for p, total in ((0, real), (1, imag)):
                    value = keep * vector[a][p] - step_size * total
                    value = value + jnp.where(here, source[(color * 2 + p) * 2 + half], 0.0)
                    out[spinor_at(spin, color, p, half)] = value
    for comp in range(2):
        low_spin = 2 + lower_source(0, comp)
        upper = [load(comp, half) for half in range(2)]
        lower = [load(low_spin, half) for half in range(2)]
        top = [load_spin(out, comp, half) for half in range(2)]
        bottom = [load_spin(out, low_spin, half) for half in range(2)]
        for mu in range(2):
            ahead = [half_spin(mu, comp, -1, upper[h], lower[h]) for h in range(2)]
            ahead = shift_plane(mu, ahead, True)
            for h in range(2):
                hopped = link_times(links, mu, h, ahead[h], False)
                top[h], bottom[h] = accumulate(top[h], bottom[h], mu, comp, -1, hopped)
            behind = [
                link_times(links, mu, h, half_spin(mu, comp, 1, upper[h], lower[h]), True)
                for h in range(2)
            ]
            behind = shift_plane(mu, behind, False)
            for h in range(2):
                top[h], bottom[h] = accumulate(top[h], bottom[h], mu, comp, 1, behind[h])
        for h in range(2):
            store_spin(out, comp, h, top[h])
            store_spin(out, low_spin, h, bottom[h])


def source_spinor(source):
    def load(spin, half):
        here = spin_mask(spin)
        return [
            tuple(jnp.where(here, source[(c * 2 + p) * 2 + half], 0.0) for p in range(2))
            for c in range(3)
        ]

    return load


def local_first_kernel(links, clover, source, out):
    local_body(source_spinor(source), links, clover, source, out)


def local_kernel(solution, links, clover, source, out):
    local_body(lambda spin, half: load_spin(solution, spin, half), links, clover, source, out)


def hops(local, links, received, comp, half):
    top, bottom = load_spin(local, comp, half), load_spin(local, 2 + comp, half)
    for mu, ahead, behind in received:
        hopped = link_times(links, mu, half, ahead(comp, half, mu, -1), False)
        top, bottom = accumulate(top, bottom, mu, comp, -1, hopped)
        top, bottom = accumulate(top, bottom, mu, comp, 1, behind(comp, half, mu, 1))
    return top, bottom


def from_halves(ref):
    return lambda comp, half, mu, sign: load_spin(ref, comp, half)


def from_source(ref):
    def load(comp, half, mu, sign):
        whole = source_spinor(ref)
        return half_spin(mu, comp, sign, whole(comp, half), whole(2 + comp, half))

    return load


def arrivals(kind, time_rank, space_rank, t_inner, t_outer, z_inner, z_outer):
    received = []
    for mu, rank, inner, outer in (
        (3, time_rank, t_inner, t_outer),
        (2, space_rank, z_inner, z_outer),
    ):
        even = is_even(rank)
        received.append((mu, kind(Pick(even, inner, outer)), kind(Pick(even, outer, inner))))
    return received


def step_body(received, time_rank, space_rank, local, links, solution, *sends):
    for comp in range(2):
        for half in range(2):
            top, bottom = hops(local, links, received, comp, half)
            store_spin(solution, comp, half, top)
            store_spin(solution, 2 + comp, half, bottom)
            for mu, rank, inner, outer in (
                (3, time_rank, *sends[:2]),
                (2, space_rank, *sends[2:]),
            ):
                ahead = half_spin(mu, comp, -1, top, bottom)
                plus = half_spin(mu, comp, 1, top, bottom)
                behind = link_times(links, mu, half, plus, True)
                store_sends(inner, outer, is_even(rank), comp, half, behind, ahead)


def step_first_kernel(sizes, time_rank, space_rank, bits, local, links, ti, to, zi, zo,
                      solution, sti, sto, szi, szo, at, bt, az, bz):
    time, space = time_rank[0], space_rank[0]
    own = source_weight(bits, time)
    later = source_weight(bits, lax.rem(time + 1, sizes[0]))
    earlier = source_weight(bits, lax.rem(time + sizes[0] - 1, sizes[0]))
    for mu, rank, inner, outer, ahead, behind, up, down, crosses in (
        (3, time_rank, ti, to, at, bt, later, earlier, time == 0),
        (2, space_rank, zi, zo, az, bz, own, own, space == 0),
    ):
        even = is_even(rank)
        down = down * hop_factor(bits, mu, crosses)
        next_links = PackedLinks(even, outer, inner, 24)
        for half in range(2):
            vector = []
            for c in range(3):
                pair = []
                for p in range(2):
                    plane = (c * 2 + p) * 2 + half
                    rows = pl.ds(plane, 8, stride=12)
                    here, there = inner[rows, :], outer[rows, :]
                    ahead[plane] = jnp.where(even, here, there) * up
                    pair.append(jnp.where(even, there, here) * down)
                vector.append(tuple(pair))
            store_spin(behind, 0, half, link_times(next_links, mu, half, vector, True))
    received = ((3, from_source(at), from_source(bt)), (2, from_source(az), from_source(bz)))
    step_body(received, time_rank, space_rank, local, links, solution, sti, sto, szi, szo)


def step_kernel(time_rank, space_rank, local, links, ti, to, zi, zo, *outs):
    received = arrivals(from_halves, time_rank, space_rank, ti, to, zi, zo)
    step_body(received, time_rank, space_rank, local, links, *outs)


def modes_kernel(modes, out):
    count = modes.shape[0] // 12
    out[...] = jnp.zeros(out.shape, out.dtype)
    for c in range(3):
        for half in range(2):
            real = modes[pl.ds(4 * c + half, count, stride=12), :]
            imag = modes[pl.ds(4 * c + 2 + half, count, stride=12), :]
            lanes = slice(half * LANES, half * LANES + LANES)
            for p, upper, lower in ((0, real, -imag), (1, imag, real)):
                for start, value in ((0, upper), (count, lower)):
                    high = value.astype(jnp.bfloat16)
                    low = (value - high.astype(F32)).astype(jnp.bfloat16)
                    out[2 * c + p, start : start + count, lanes] = high
                    out[2 * c + p, 128 + start : 128 + start + count, lanes] = low


def last_kernel(time_rank, space_rank, local, links, ti, to, zi, zo, modes, out, rows):
    received = arrivals(from_halves, time_rank, space_rank, ti, to, zi, zo)
    for comp in range(2):
        for half in range(2):
            pair = hops(local, links, received, comp, half)
            for spin, value in zip((comp, 2 + comp), pair, strict=True):
                for c in range(3):
                    for p in range(2):
                        rows[2 * c + p, 8 * spin : 8 * spin + 8, half * LANES : half * LANES + LANES] = value[c][p]
    total = None
    for plane in range(6):
        value = rows[plane]
        high = value.astype(jnp.bfloat16)
        low = (value - high.astype(F32)).astype(jnp.bfloat16)
        product = lax.dot_general(
            jnp.concatenate([high, low], 0),
            modes[plane],
            (((1,), (1,)), ((), ())),
            preferred_element_type=F32,
        )
        total = product if total is None else total + product
    total = total[:32, :128] + (total[:32, 128:] + total[32:, :128])
    for spin in range(4):
        out[pl.ds(spin, 8, stride=4), :] = total[8 * spin : 8 * spin + 8, : out.shape[1]]


def sum_kernel(parts, out, copies):
    total = jnp.sum(parts[...], axis=0, keepdims=True)
    out[...] = total
    copies[...] = jnp.broadcast_to(total, copies.shape)


def correlate_kernel(time_rank, rows, partner, out):
    size = rows.shape[1]
    onehot = (
        partner[...] == lax.broadcasted_iota(jnp.int32, (size, size), 0)
    ).astype(F32)
    contract = (((1,), (1,)), ((), ()))
    own = jnp.broadcast_to(rows[pl.ds(time_rank[0], 1), :], (8, size))
    weighted = lax.dot_general(
        own, onehot, contract, precision=lax.Precision.HIGHEST, preferred_element_type=F32
    )
    found = lax.dot_general(
        weighted, rows[...], contract, precision=lax.Precision.HIGHEST, preferred_element_type=F32
    )
    out[...] = found[:1]


def call(kernel, outs, flops, scalars, *args, scratch=()):
    vmem = pl.BlockSpec(memory_space=pltpu.VMEM)
    smem = pl.BlockSpec(memory_space=pltpu.SMEM)
    single = not isinstance(outs, (list, tuple))
    shapes = [outs] if single else list(outs)
    moved = 4 * sum(a.size for a in args) + 4 * sum(s.size for s in shapes)
    out = pl.pallas_call(
        kernel,
        out_shape=outs,
        in_specs=[smem] * len(scalars) + [vmem] * len(args),
        out_specs=vmem if single else [vmem] * len(shapes),
        scratch_shapes=scratch,
        compiler_params=pltpu.CompilerParams(vmem_limit_bytes=16 << 20),
        cost_estimate=pl.CostEstimate(flops=flops, bytes_accessed=moved, transcendentals=0),
    )(*scalars, *args)
    return out


def vectors(count):
    return jax.ShapeDtypeStruct((count, 8, LANES), F32)


def exchange(t_inner, t_outer, z_inner, z_outer):
    def swap(axis, shift):
        size = lax.axis_size(axis)
        pairs = [((i + shift) % size, (i + 1 + shift) % size) for i in range(0, size, 2)]
        return pairs + [(j, i) for i, j in pairs]

    zi = lax.ppermute(z_inner, "space", swap("space", 0))
    zo = lax.ppermute(z_outer, "space", swap("space", 1))
    ti = lax.ppermute(t_inner, "tm", swap("tm", 0))
    to = lax.ppermute(t_outer, "tm", swap("tm", 1))
    return ti, to, zi, zo


def mesh_ranks():
    return tuple(lax.axis_index(name).astype(jnp.int32).reshape(1) for name in ("tm", "space"))


def partial_rows(noise_field, gauge_links, clover, eigvecs, dilution, boundary):
    count = eigvecs.shape[0]
    noise = noise_field.reshape(-1, LANES)
    links_in = gauge_links.reshape(-1, LANES)
    clover = clover.reshape(-1, LANES)
    modes_in = eigvecs.reshape(-1, LANES)
    ranks = mesh_ranks()
    sizes = (lax.axis_size("tm"), lax.axis_size("space"))
    bits = jnp.concatenate([boundary, dilution])

    def prepare(*refs):
        prepare_kernel(sizes, *refs)

    def step_first(*refs):
        step_first_kernel(sizes, *refs)

    packed = jnp.concatenate([noise, links_in[links_in.shape[0] // 2 :]])
    sends = (packed,) * 4
    solution = None
    for iteration in range(ITERS):
        arrived = exchange(*sends)
        if iteration == 0:
            links, source = call(
                prepare,
                [jax.ShapeDtypeStruct(links_in.shape, F32), vectors(12)],
                10**6,
                (*ranks, bits),
                noise,
                links_in,
            )
            local = call(local_first_kernel, vectors(48), 5 * 10**6, (), links, clover, source)
            modes = call(
                modes_kernel,
                jax.ShapeDtypeStruct((6, 256, 256), jnp.bfloat16),
                10**6,
                (),
                modes_in,
            )
        else:
            local = call(local_kernel, vectors(48), 5 * 10**6, (), solution, links, clover, source)
        if iteration < ITERS - 1:
            first = iteration == 0
            solution, *sends = call(
                step_first if first else step_kernel,
                [vectors(48)] + [vectors(24)] * 4,
                3 * 10**6,
                (*ranks, bits) if first else ranks,
                local, links, *arrived,
                scratch=[pltpu.VMEM((12, 8, LANES), F32)] * 4 if first else (),
            )
        else:
            partial_sums = call(
                last_kernel,
                jax.ShapeDtypeStruct((32, 2 * count), F32),
                10**7,
                ranks,
                local, links, *arrived, modes,
                scratch=[pltpu.VMEM((6, 32, 256), F32)],
            )
    return partial_sums


def shards(noise_field, gauge_links, clover, eigvecs, partner, dilution, boundary):
    count = eigvecs.shape[0]
    partial_sums = partial_rows(
        noise_field, gauge_links, clover, eigvecs, dilution, boundary
    )
    parts = lax.all_to_all(partial_sums, "space", 0, 0, tiled=True)
    times, ranks = lax.axis_size("tm"), mesh_ranks()[:1]
    row, copies = call(
        sum_kernel,
        [jax.ShapeDtypeStruct((n, 2 * count), F32) for n in (1, times)],
        10**4,
        (),
        parts,
    )
    rows = lax.all_to_all(copies, "tm", 0, 0, tiled=True)
    both = jnp.concatenate([partner, partner + count]).reshape(1, 2 * count)
    correlator = call(
        correlate_kernel, jax.ShapeDtypeStruct((1, times), F32), 10**5, ranks, rows, both
    )
    return row.reshape(1, 1, 2 * count), correlator.reshape(1, 1, times)


def solution(mesh):
    return jax.shard_map(
        shards,
        mesh=mesh,
        in_specs=(
            P(None, "tm", "space", None, None),
            P(None, None, "tm", "space", None, None),
            P(None, None, "tm", "space", None, None),
            P(None, "tm", "space", None, None),
            P(),
            P(),
            P(),
        ),
        out_specs=(P("space", "tm", None), P("space", "tm", None)),
        check_vma=False,
    )
```

```python
import jax
import jax.numpy as jnp
from jax import lax
from jax.experimental import pallas as pl
from jax.experimental.pallas import tpu as pltpu
from jax.sharding import PartitionSpec as P

ITERS = 4
DILUTE = 4
SIDE = 16
LANES = 128
diag_term = 4.1
step_size = 0.2
F32 = jnp.float32

twist_table = (
    (((1, 0, -1), (0, 0, -1)), ((1, 0, 1), (0, 0, 1))),
    (((1, -1, 0), (0, 1, 0)), ((1, 1, 0), (0, -1, 0))),
    (((0, 0, -1), (1, 0, 1)), ((0, 0, 1), (1, 0, -1))),
    (((0, 1, 0), (1, 1, 0)), ((0, 1, 0), (1, 1, 0))),
)


def add_scaled(pair, sign, coef, other):
    real_coef, imag_coef = coef
    if imag_coef == 0:
        if sign * real_coef > 0:
            return (pair[0] + other[0], pair[1] + other[1])
        return (pair[0] - other[0], pair[1] - other[1])
    if sign * imag_coef > 0:
        return (pair[0] - other[1], pair[1] + other[0])
    return (pair[0] + other[1], pair[1] - other[0])


def row8(ref, row):
    if isinstance(ref, PackedLinks):
        return jnp.where(ref.first, *(row8(side, row + base + 24) for side, base in ref.sides))
    return ref[pl.ds(row, 8, stride=0), :]


class PackedLinks:
    def __init__(self, first, *sides):
        self.first, self.sides = first, sides


def link_times(links, mu, half, vector, adjoint):
    out = []
    for i in range(3):
        real, imag = None, None
        for k in range(3):
            row, col = (k, i) if adjoint else (i, k)
            base = ((mu * 3 + row) * 6 + 2 * col) * 2 + half
            mr, mi = row8(links, base), row8(links, base + 2)
            vr, vi = vector[k]
            if adjoint:
                r, m = mr * vr + mi * vi, mr * vi - mi * vr
            else:
                r, m = mr * vr - mi * vi, mr * vi + mi * vr
            real = r if real is None else real + r
            imag = m if imag is None else imag + m
        out.append((real, imag))
    return out


def spinor_at(spin, color, part, half):
    return ((spin * 3 + color) * 2 + part) * 2 + half


def load_spin(ref, spin, half):
    return [
        tuple(ref[spinor_at(spin, c, p, half)] for p in range(2)) for c in range(3)
    ]


def store_spin(ref, spin, half, value):
    for c in range(3):
        for p in range(2):
            ref[spinor_at(spin, c, p, half)] = value[c][p]


def half_spin(mu, comp, sign, upper, lower):
    _, real_coef, imag_coef = twist_table[mu][0][comp]
    return [
        add_scaled(upper[c], sign, (real_coef, imag_coef), lower[c]) for c in range(3)
    ]


def lower_target(mu, comp):
    for target in range(2):
        source, real_coef, imag_coef = twist_table[mu][1][target]
        if source == comp:
            return target, (real_coef, imag_coef)
    raise ValueError


def lower_source(mu, comp):
    return twist_table[mu][0][comp][0]


def accumulate(top, bottom, mu, comp, sign, hopped):
    _, coef = lower_target(mu, comp)
    top = [(top[c][0] + hopped[c][0], top[c][1] + hopped[c][1]) for c in range(3)]
    bottom = [add_scaled(bottom[c], sign, coef, hopped[c]) for c in range(3)]
    return top, bottom


def source_rows(shape):
    return lax.broadcasted_iota(jnp.int32, shape, 0)


def spin_mask(spin):
    return source_rows((8, LANES)) % 4 == spin


class Pick:
    def __init__(self, first, *sides):
        self.first, self.sides = first, sides

    def __getitem__(self, index):
        return jnp.where(self.first, *(ref[base + index] for ref, base in self.sides))


def neighbours(time_rank, space_rank, ti, to, zi, zo):
    half = zi.shape[0] // 2
    return (
        (3, is_even(time_rank), ((ti, 0), (to, 0)), ((to, 0), (ti, 0))),
        (2, is_even(space_rank), ((zi, half), (zo, 0)), ((zo, 0), (zi, 0))),
    )


def is_even(rank):
    return jnp.full((8, LANES), rank[0], jnp.int32) % 2 == 0


def store_sends(inner, outer, even, comp, half, behind, ahead):
    for c in range(3):
        for p in range(2):
            up, down = behind[c][p], ahead[c][p]
            inner[spinor_at(comp, c, p, half)] = jnp.where(even, up, down)
            outer[spinor_at(comp, c, p, half)] = jnp.where(even, down, up)


def source_weight(bits, time):
    row = source_rows((8, LANES))
    weight = jnp.zeros((8, LANES), F32)
    for j in range(8):
        on = jnp.where(time % DILUTE == bits[4 + j], step_size, 0.0)
        weight = jnp.where(row == j, on, weight)
    return weight


def hop_factor(bits, mu, crosses):
    phase = (1 - 2 * bits[mu]).astype(F32) * (0.5 * step_size)
    return jnp.where(crosses, phase, 0.5 * step_size)


def prepare_kernel(sizes, time_rank, space_rank, bits, noise, links_in, links, source):
    lane = lax.broadcasted_iota(jnp.int32, (8, LANES), 1)
    row = lax.broadcasted_iota(jnp.int32, (8, LANES), 0)
    at_x = hop_factor(bits, 0, lane % SIDE == SIDE - 1)
    at_y = hop_factor(bits, 1, (lane >= LANES - SIDE) & (row % 2 == 1))
    at_z = jnp.full((8, LANES), hop_factor(bits, 2, space_rank[0] == sizes[1] - 1))
    at_t = jnp.full((8, LANES), hop_factor(bits, 3, time_rank[0] == sizes[0] - 1))
    scales = (at_x, at_y, at_z, at_t)
    for block in range(18):
        first, last = (block * 8) // 36, (block * 8 + 7) // 36
        scale = scales[first]
        if last != first:
            scale = jnp.where(row + block * 8 >= last * 36, scales[last], scale)
        links[block * 8 : block * 8 + 8, :] = links_in[block * 8 : block * 8 + 8, :] * scale
    weight = source_weight(bits, time_rank[0])
    for plane in range(12):
        source[plane] = noise[pl.ds(plane, 8, stride=12), :] * weight


def shift_x(value, forward):
    lane = lax.broadcasted_iota(jnp.int32, (8, LANES), 1) % SIDE
    if forward:
        return jnp.where(
            lane == SIDE - 1,
            pltpu.roll(value, SIDE - 1, 1),
            pltpu.roll(value, LANES - 1, 1),
        )
    return jnp.where(
        lane == 0, pltpu.roll(value, LANES - SIDE + 1, 1), pltpu.roll(value, 1, 1)
    )


def shift_y(low, high, forward):
    lane = lax.broadcasted_iota(jnp.int32, (8, LANES), 1)
    if forward:
        a, b = pltpu.roll(low, LANES - SIDE, 1), pltpu.roll(high, LANES - SIDE, 1)
        keep = lane < LANES - SIDE
    else:
        a, b = pltpu.roll(low, SIDE, 1), pltpu.roll(high, SIDE, 1)
        keep = lane >= SIDE
    return jnp.where(keep, a, b), jnp.where(keep, b, a)


def shift_plane(mu, pair_of_halves, forward):
    moved = ([], [])
    for c in range(3):
        parts = ([], [])
        for p in range(2):
            low, high = pair_of_halves[0][c][p], pair_of_halves[1][c][p]
            if mu == 0:
                low, high = shift_x(low, forward), shift_x(high, forward)
            else:
                low, high = shift_y(low, high, forward)
            parts[0].append(low)
            parts[1].append(high)
        moved[0].append(tuple(parts[0]))
        moved[1].append(tuple(parts[1]))
    return moved


def local_body(load, links, clover, source, out):
    for chiral in range(2):
        for half in range(2):
            vector = load(2 * chiral, half) + load(2 * chiral + 1, half)
            for a in range(6):
                real, imag = None, None
                for b in range(6):
                    base = ((chiral * 6 + a) * 12 + 2 * b) * 2 + half
                    mr, mi = row8(clover, base), row8(clover, base + 2)
                    vr, vi = vector[b]
                    r, m = mr * vr - mi * vi, mr * vi + mi * vr
                    real = r if real is None else real + r
                    imag = m if imag is None else imag + m
                spin, color = 2 * chiral + a // 3, a % 3
                here = spin_mask(spin)
                keep = 1.0 - step_size * diag_term
                for p, total in ((0, real), (1, imag)):
                    value = keep * vector[a][p] - step_size * total
                    value = value + jnp.where(here, source[(color * 2 + p) * 2 + half], 0.0)
                    out[spinor_at(spin, color, p, half)] = value
    for comp in range(2):
        low_spin = 2 + lower_source(0, comp)
        upper = [load(comp, half) for half in range(2)]
        lower = [load(low_spin, half) for half in range(2)]
        top = [load_spin(out, comp, half) for half in range(2)]
        bottom = [load_spin(out, low_spin, half) for half in range(2)]
        for mu in range(2):
            ahead = [half_spin(mu, comp, -1, upper[h], lower[h]) for h in range(2)]
            ahead = shift_plane(mu, ahead, True)
            for h in range(2):
                hopped = link_times(links, mu, h, ahead[h], False)
                top[h], bottom[h] = accumulate(top[h], bottom[h], mu, comp, -1, hopped)
            behind = [
                link_times(links, mu, h, half_spin(mu, comp, 1, upper[h], lower[h]), True)
                for h in range(2)
            ]
            behind = shift_plane(mu, behind, False)
            for h in range(2):
                top[h], bottom[h] = accumulate(top[h], bottom[h], mu, comp, 1, behind[h])
        for h in range(2):
            store_spin(out, comp, h, top[h])
            store_spin(out, low_spin, h, bottom[h])


def source_spinor(source):
    def load(spin, half):
        here = spin_mask(spin)
        return [
            tuple(jnp.where(here, source[(c * 2 + p) * 2 + half], 0.0) for p in range(2))
            for c in range(3)
        ]

    return load


def local_first_kernel(links, clover, source, out):
    local_body(source_spinor(source), links, clover, source, out)


def local_kernel(solution, links, clover, source, out):
    local_body(lambda spin, half: load_spin(solution, spin, half), links, clover, source, out)


def hops(local, links, received, comp, half):
    top, bottom = load_spin(local, comp, half), load_spin(local, 2 + comp, half)
    for mu, ahead, behind in received:
        hopped = link_times(links, mu, half, ahead(comp, half, mu, -1), False)
        top, bottom = accumulate(top, bottom, mu, comp, -1, hopped)
        top, bottom = accumulate(top, bottom, mu, comp, 1, behind(comp, half, mu, 1))
    return top, bottom


def from_halves(ref):
    return lambda comp, half, mu, sign: load_spin(ref, comp, half)


def from_source(ref):
    def load(comp, half, mu, sign):
        whole = source_spinor(ref)
        return half_spin(mu, comp, sign, whole(comp, half), whole(2 + comp, half))

    return load


def arrivals(*refs):
    return [
        (mu, from_halves(Pick(even, *after)), from_halves(Pick(even, *before)))
        for mu, even, after, before in neighbours(*refs)
    ]


def step_body(received, time_rank, space_rank, local, links, solution, *sends):
    for comp in range(2):
        for half in range(2):
            top, bottom = hops(local, links, received, comp, half)
            store_spin(solution, comp, half, top)
            store_spin(solution, 2 + comp, half, bottom)
            for mu, rank, inner, outer in (
                (3, time_rank, *sends[:2]),
                (2, space_rank, *sends[2:]),
            ):
                ahead = half_spin(mu, comp, -1, top, bottom)
                plus = half_spin(mu, comp, 1, top, bottom)
                behind = link_times(links, mu, half, plus, True)
                store_sends(inner, outer, is_even(rank), comp, half, behind, ahead)


def step_first_kernel(sizes, time_rank, space_rank, bits, local, links, ti, to, zi, zo,
                      solution, sti, sto, szi, szo, at, bt, az, bz):
    time, space = time_rank[0], space_rank[0]
    own = source_weight(bits, time)
    later = source_weight(bits, lax.rem(time + 1, sizes[0]))
    earlier = source_weight(bits, lax.rem(time + sizes[0] - 1, sizes[0]))
    blocks = neighbours(time_rank, space_rank, ti, to, zi, zo)
    for (mu, even, after, before), ahead, behind, up, down, crosses in (
        (blocks[0], at, bt, later, earlier, time == 0),
        (blocks[1], az, bz, own, own, space == 0),
    ):
        down = down * hop_factor(bits, mu, crosses)
        for half in range(2):
            vector = []
            for c in range(3):
                pair = []
                for p in range(2):
                    plane = (c * 2 + p) * 2 + half
                    next_block, last_block = (
                        jnp.where(even, *(ref[pl.ds(base + plane, 8, stride=12), :] for ref, base in sides))
                        for sides in (after, before)
                    )
                    ahead[plane] = next_block * up
                    pair.append(last_block * down)
                vector.append(tuple(pair))
            moved = link_times(PackedLinks(even, *before), mu, half, vector, True)
            store_spin(behind, 0, half, moved)
    received = ((3, from_source(at), from_source(bt)), (2, from_source(az), from_source(bz)))
    step_body(received, time_rank, space_rank, local, links, solution, sti, sto, szi, szo)


def step_kernel(time_rank, space_rank, local, links, ti, to, zi, zo, *outs):
    received = arrivals(time_rank, space_rank, ti, to, zi, zo)
    step_body(received, time_rank, space_rank, local, links, *outs)


def modes_kernel(modes, out):
    count = modes.shape[0] // 12
    out[...] = jnp.zeros(out.shape, out.dtype)
    for c in range(3):
        for half in range(2):
            real = modes[pl.ds(4 * c + half, count, stride=12), :]
            imag = modes[pl.ds(4 * c + 2 + half, count, stride=12), :]
            lanes = slice(half * LANES, half * LANES + LANES)
            for p, upper, lower in ((0, real, -imag), (1, imag, real)):
                for start, value in ((0, upper), (count, lower)):
                    high = value.astype(jnp.bfloat16)
                    low = (value - high.astype(F32)).astype(jnp.bfloat16)
                    out[2 * c + p, start : start + count, lanes] = high
                    out[2 * c + p, 128 + start : 128 + start + count, lanes] = low


def last_kernel(time_rank, space_rank, local, links, ti, to, zi, zo, modes, out, rows):
    received = arrivals(time_rank, space_rank, ti, to, zi, zo)
    for comp in range(2):
        for half in range(2):
            pair = hops(local, links, received, comp, half)
            for spin, value in zip((comp, 2 + comp), pair, strict=True):
                for c in range(3):
                    for p in range(2):
                        rows[2 * c + p, 8 * spin : 8 * spin + 8, half * LANES : half * LANES + LANES] = value[c][p]
    total = None
    for plane in range(6):
        value = rows[plane]
        high = value.astype(jnp.bfloat16)
        low = (value - high.astype(F32)).astype(jnp.bfloat16)
        product = lax.dot_general(
            jnp.concatenate([high, low], 0),
            modes[plane],
            (((1,), (1,)), ((), ())),
            preferred_element_type=F32,
        )
        total = product if total is None else total + product
    total = total[:32, :128] + (total[:32, 128:] + total[32:, :128])
    for spin in range(4):
        out[pl.ds(spin, 8, stride=4), :] = total[8 * spin : 8 * spin + 8, : out.shape[1]]


def sum_kernel(parts, out, copies):
    total = jnp.sum(parts[...], axis=0, keepdims=True)
    out[...] = total
    copies[...] = jnp.broadcast_to(total, copies.shape)


def correlate_kernel(time_rank, rows, partner, out):
    size = rows.shape[1]
    onehot = (
        partner[...] == lax.broadcasted_iota(jnp.int32, (size, size), 0)
    ).astype(F32)
    contract = (((1,), (1,)), ((), ()))
    own = jnp.broadcast_to(rows[pl.ds(time_rank[0], 1), :], (8, size))
    weighted = lax.dot_general(
        own, onehot, contract, precision=lax.Precision.HIGHEST, preferred_element_type=F32
    )
    found = lax.dot_general(
        weighted, rows[...], contract, precision=lax.Precision.HIGHEST, preferred_element_type=F32
    )
    out[...] = found[:1]


def call(kernel, outs, flops, scalars, *args, scratch=()):
    vmem = pl.BlockSpec(memory_space=pltpu.VMEM)
    smem = pl.BlockSpec(memory_space=pltpu.SMEM)
    single = not isinstance(outs, (list, tuple))
    shapes = [outs] if single else list(outs)
    moved = 4 * sum(a.size for a in args) + 4 * sum(s.size for s in shapes)
    out = pl.pallas_call(
        kernel,
        out_shape=outs,
        in_specs=[smem] * len(scalars) + [vmem] * len(args),
        out_specs=vmem if single else [vmem] * len(shapes),
        scratch_shapes=scratch,
        compiler_params=pltpu.CompilerParams(vmem_limit_bytes=16 << 20),
        cost_estimate=pl.CostEstimate(flops=flops, bytes_accessed=moved, transcendentals=0),
    )(*scalars, *args)
    return out


def vectors(count):
    return jax.ShapeDtypeStruct((count, 8, LANES), F32)


def exchange(t_inner, t_outer, z_inner, z_outer):
    def swap(axis, shift):
        size = lax.axis_size(axis)
        pairs = [((i + shift) % size, (i + 1 + shift) % size) for i in range(0, size, 2)]
        return pairs + [(j, i) for i, j in pairs]

    pairs = [[i, i + 1] for i in range(0, lax.axis_size("space"), 2)]
    zi = lax.all_gather(z_inner, "space", axis_index_groups=pairs, tiled=True)
    zo = lax.ppermute(z_outer, "space", swap("space", 1))
    ti = lax.ppermute(t_inner, "tm", swap("tm", 0))
    to = lax.ppermute(t_outer, "tm", swap("tm", 1))
    return ti, to, zi, zo


def mesh_ranks():
    return tuple(lax.axis_index(name).astype(jnp.int32).reshape(1) for name in ("tm", "space"))


def partial_rows(noise_field, gauge_links, clover, eigvecs, dilution, boundary):
    count = eigvecs.shape[0]
    noise = noise_field.reshape(-1, LANES)
    links_in = gauge_links.reshape(-1, LANES)
    clover = clover.reshape(-1, LANES)
    modes_in = eigvecs.reshape(-1, LANES)
    ranks = mesh_ranks()
    sizes = (lax.axis_size("tm"), lax.axis_size("space"))
    bits = jnp.concatenate([boundary, dilution])

    def prepare(*refs):
        prepare_kernel(sizes, *refs)

    def step_first(*refs):
        step_first_kernel(sizes, *refs)

    packed = jnp.concatenate([noise, links_in[links_in.shape[0] // 2 :]])
    sends = (packed,) * 4
    solution = None
    for iteration in range(ITERS):
        arrived = exchange(*sends)
        if iteration == 0:
            links, source = call(
                prepare,
                [jax.ShapeDtypeStruct(links_in.shape, F32), vectors(12)],
                10**6,
                (*ranks, bits),
                noise,
                links_in,
            )
            local = call(local_first_kernel, vectors(48), 5 * 10**6, (), links, clover, source)
            modes = call(
                modes_kernel,
                jax.ShapeDtypeStruct((6, 256, 256), jnp.bfloat16),
                10**6,
                (),
                modes_in,
            )
        else:
            local = call(local_kernel, vectors(48), 5 * 10**6, (), solution, links, clover, source)
        if iteration < ITERS - 1:
            first = iteration == 0
            solution, *sends = call(
                step_first if first else step_kernel,
                [vectors(48)] + [vectors(24)] * 4,
                3 * 10**6,
                (*ranks, bits) if first else ranks,
                local, links, *arrived,
                scratch=[pltpu.VMEM((12, 8, LANES), F32)] * 4 if first else (),
            )
        else:
            partial_sums = call(
                last_kernel,
                jax.ShapeDtypeStruct((32, 2 * count), F32),
                10**7,
                ranks,
                local, links, *arrived, modes,
                scratch=[pltpu.VMEM((6, 32, 256), F32)],
            )
    return partial_sums


def shards(noise_field, gauge_links, clover, eigvecs, partner, dilution, boundary):
    count = eigvecs.shape[0]
    partial_sums = partial_rows(
        noise_field, gauge_links, clover, eigvecs, dilution, boundary
    )
    both = jnp.concatenate([partner, partner + count]).reshape(1, 2 * count)
    both, partial_sums = lax.optimization_barrier((both, partial_sums))
    parts = lax.all_to_all(partial_sums, "space", 0, 0, tiled=True)
    times, ranks = lax.axis_size("tm"), mesh_ranks()[:1]
    row, copies = call(
        sum_kernel,
        [jax.ShapeDtypeStruct((n, 2 * count), F32) for n in (1, times)],
        10**4,
        (),
        parts,
    )
    rows = lax.all_to_all(copies, "tm", 0, 0, tiled=True)
    correlator = call(
        correlate_kernel, jax.ShapeDtypeStruct((1, times), F32), 10**5, ranks, rows, both
    )
    return row.reshape(1, 1, 2 * count), correlator.reshape(1, 1, times)


def solution(mesh):
    return jax.shard_map(
        shards,
        mesh=mesh,
        in_specs=(
            P(None, "tm", "space", None, None),
            P(None, None, "tm", "space", None, None),
            P(None, None, "tm", "space", None, None),
            P(None, "tm", "space", None, None),
            P(),
            P(),
            P(),
        ),
        out_specs=(P("space", "tm", None), P("space", "tm", None)),
        check_vma=False,
    )
```

```python
import jax
import jax.numpy as jnp
from jax import lax
from jax.experimental import pallas as pl
from jax.experimental.pallas import tpu as pltpu
from jax.sharding import PartitionSpec as P

ITERS = 4
DILUTE = 4
SIDE = 16
LANES = 128
diag_term = 4.1
step_size = 0.2
F32 = jnp.float32

twist_table = (
    (((1, 0, -1), (0, 0, -1)), ((1, 0, 1), (0, 0, 1))),
    (((1, -1, 0), (0, 1, 0)), ((1, 1, 0), (0, -1, 0))),
    (((0, 0, -1), (1, 0, 1)), ((0, 0, 1), (1, 0, -1))),
    (((0, 1, 0), (1, 1, 0)), ((0, 1, 0), (1, 1, 0))),
)


def add_scaled(pair, sign, coef, other):
    real_coef, imag_coef = coef
    if imag_coef == 0:
        if sign * real_coef > 0:
            return (pair[0] + other[0], pair[1] + other[1])
        return (pair[0] - other[0], pair[1] - other[1])
    if sign * imag_coef > 0:
        return (pair[0] - other[1], pair[1] + other[0])
    return (pair[0] + other[1], pair[1] - other[0])


def row8(ref, row):
    if isinstance(ref, PackedLinks):
        return jnp.where(ref.first, *(row8(side, row + base + 24) for side, base in ref.sides))
    return ref[pl.ds(row, 8, stride=0), :]


class PackedLinks:
    def __init__(self, first, *sides):
        self.first, self.sides = first, sides


def link_times(links, mu, half, vector, adjoint):
    out = []
    for i in range(3):
        real, imag = None, None
        for k in range(3):
            row, col = (k, i) if adjoint else (i, k)
            base = ((mu * 3 + row) * 6 + 2 * col) * 2 + half
            mr, mi = row8(links, base), row8(links, base + 2)
            vr, vi = vector[k]
            if adjoint:
                r, m = mr * vr + mi * vi, mr * vi - mi * vr
            else:
                r, m = mr * vr - mi * vi, mr * vi + mi * vr
            real = r if real is None else real + r
            imag = m if imag is None else imag + m
        out.append((real, imag))
    return out


def spinor_at(spin, color, part, half):
    return ((spin * 3 + color) * 2 + part) * 2 + half


def load_spin(ref, spin, half):
    return [
        tuple(ref[spinor_at(spin, c, p, half)] for p in range(2)) for c in range(3)
    ]


def store_spin(ref, spin, half, value):
    for c in range(3):
        for p in range(2):
            ref[spinor_at(spin, c, p, half)] = value[c][p]


def half_spin(mu, comp, sign, upper, lower):
    _, real_coef, imag_coef = twist_table[mu][0][comp]
    return [
        add_scaled(upper[c], sign, (real_coef, imag_coef), lower[c]) for c in range(3)
    ]


def lower_target(mu, comp):
    for target in range(2):
        source, real_coef, imag_coef = twist_table[mu][1][target]
        if source == comp:
            return target, (real_coef, imag_coef)
    raise ValueError


def lower_source(mu, comp):
    return twist_table[mu][0][comp][0]


def accumulate(top, bottom, mu, comp, sign, hopped):
    _, coef = lower_target(mu, comp)
    top = [(top[c][0] + hopped[c][0], top[c][1] + hopped[c][1]) for c in range(3)]
    bottom = [add_scaled(bottom[c], sign, coef, hopped[c]) for c in range(3)]
    return top, bottom


def source_rows(shape):
    return lax.broadcasted_iota(jnp.int32, shape, 0)


def spin_mask(spin):
    return source_rows((8, LANES)) % 4 == spin


class Pick:
    def __init__(self, first, *sides):
        self.first, self.sides = first, sides

    def __getitem__(self, index):
        return jnp.where(self.first, *(ref[base + index] for ref, base in self.sides))


def neighbours(time_rank, space_rank, ti, to, zi, zo):
    half = zi.shape[0] // 2
    return (
        (3, is_even(time_rank), ((ti, 0), (to, 0)), ((to, 0), (ti, 0))),
        (2, is_even(space_rank), ((zi, half), (zo, 0)), ((zo, 0), (zi, 0))),
    )


def is_even(rank):
    return jnp.full((8, LANES), rank[0], jnp.int32) % 2 == 0


def store_sends(inner, outer, even, comp, half, behind, ahead):
    for c in range(3):
        for p in range(2):
            up, down = behind[c][p], ahead[c][p]
            inner[spinor_at(comp, c, p, half)] = jnp.where(even, up, down)
            outer[spinor_at(comp, c, p, half)] = jnp.where(even, down, up)


def source_weight(bits, time):
    row = source_rows((8, LANES))
    weight = jnp.zeros((8, LANES), F32)
    for j in range(8):
        on = jnp.where(time % DILUTE == bits[4 + j], step_size, 0.0)
        weight = jnp.where(row == j, on, weight)
    return weight


def hop_factor(bits, mu, crosses):
    phase = (1 - 2 * bits[mu]).astype(F32) * (0.5 * step_size)
    return jnp.where(crosses, phase, 0.5 * step_size)


def prepare_kernel(sizes, time_rank, space_rank, bits, packed, links, source):
    lane = lax.broadcasted_iota(jnp.int32, (8, LANES), 1)
    row = lax.broadcasted_iota(jnp.int32, (8, LANES), 0)
    at_x = hop_factor(bits, 0, lane % SIDE == SIDE - 1)
    at_y = hop_factor(bits, 1, (lane >= LANES - SIDE) & (row % 2 == 1))
    at_z = jnp.full((8, LANES), hop_factor(bits, 2, space_rank[0] == sizes[1] - 1))
    at_t = jnp.full((8, LANES), hop_factor(bits, 3, time_rank[0] == sizes[0] - 1))
    scales = (at_x, at_y, at_z, at_t)
    for block in range(18):
        first, last = (block * 8) // 36, (block * 8 + 7) // 36
        scale = scales[first]
        if last != first:
            scale = jnp.where(row + block * 8 >= last * 36, scales[last], scale)
        from_row = 8 * block + (168 if block < 9 else 24)
        links[block * 8 : block * 8 + 8, :] = packed[from_row : from_row + 8, :] * scale
    weight = source_weight(bits, time_rank[0])
    for plane in range(12):
        source[plane] = packed[pl.ds(plane, 8, stride=12), :] * weight


def shift_x(value, forward):
    lane = lax.broadcasted_iota(jnp.int32, (8, LANES), 1) % SIDE
    if forward:
        return jnp.where(
            lane == SIDE - 1,
            pltpu.roll(value, SIDE - 1, 1),
            pltpu.roll(value, LANES - 1, 1),
        )
    return jnp.where(
        lane == 0, pltpu.roll(value, LANES - SIDE + 1, 1), pltpu.roll(value, 1, 1)
    )


def shift_y(low, high, forward):
    lane = lax.broadcasted_iota(jnp.int32, (8, LANES), 1)
    if forward:
        a, b = pltpu.roll(low, LANES - SIDE, 1), pltpu.roll(high, LANES - SIDE, 1)
        keep = lane < LANES - SIDE
    else:
        a, b = pltpu.roll(low, SIDE, 1), pltpu.roll(high, SIDE, 1)
        keep = lane >= SIDE
    return jnp.where(keep, a, b), jnp.where(keep, b, a)


def shift_plane(mu, pair_of_halves, forward):
    moved = ([], [])
    for c in range(3):
        parts = ([], [])
        for p in range(2):
            low, high = pair_of_halves[0][c][p], pair_of_halves[1][c][p]
            if mu == 0:
                low, high = shift_x(low, forward), shift_x(high, forward)
            else:
                low, high = shift_y(low, high, forward)
            parts[0].append(low)
            parts[1].append(high)
        moved[0].append(tuple(parts[0]))
        moved[1].append(tuple(parts[1]))
    return moved


def local_body(load, links, clover, source, out):
    for chiral in range(2):
        for half in range(2):
            vector = load(2 * chiral, half) + load(2 * chiral + 1, half)
            for a in range(6):
                real, imag = None, None
                for b in range(6):
                    base = ((chiral * 6 + a) * 12 + 2 * b) * 2 + half
                    mr, mi = row8(clover, base), row8(clover, base + 2)
                    vr, vi = vector[b]
                    r, m = mr * vr - mi * vi, mr * vi + mi * vr
                    real = r if real is None else real + r
                    imag = m if imag is None else imag + m
                spin, color = 2 * chiral + a // 3, a % 3
                here = spin_mask(spin)
                keep = 1.0 - step_size * diag_term
                for p, total in ((0, real), (1, imag)):
                    value = keep * vector[a][p] - step_size * total
                    value = value + jnp.where(here, source[(color * 2 + p) * 2 + half], 0.0)
                    out[spinor_at(spin, color, p, half)] = value
    for comp in range(2):
        low_spin = 2 + lower_source(0, comp)
        upper = [load(comp, half) for half in range(2)]
        lower = [load(low_spin, half) for half in range(2)]
        top = [load_spin(out, comp, half) for half in range(2)]
        bottom = [load_spin(out, low_spin, half) for half in range(2)]
        for mu in range(2):
            ahead = [half_spin(mu, comp, -1, upper[h], lower[h]) for h in range(2)]
            ahead = shift_plane(mu, ahead, True)
            for h in range(2):
                hopped = link_times(links, mu, h, ahead[h], False)
                top[h], bottom[h] = accumulate(top[h], bottom[h], mu, comp, -1, hopped)
            behind = [
                link_times(links, mu, h, half_spin(mu, comp, 1, upper[h], lower[h]), True)
                for h in range(2)
            ]
            behind = shift_plane(mu, behind, False)
            for h in range(2):
                top[h], bottom[h] = accumulate(top[h], bottom[h], mu, comp, 1, behind[h])
        for h in range(2):
            store_spin(out, comp, h, top[h])
            store_spin(out, low_spin, h, bottom[h])


def source_spinor(source):
    def load(spin, half):
        here = spin_mask(spin)
        return [
            tuple(jnp.where(here, source[(c * 2 + p) * 2 + half], 0.0) for p in range(2))
            for c in range(3)
        ]

    return load


def local_first_kernel(links, clover, source, out):
    local_body(source_spinor(source), links, clover, source, out)


def local_kernel(solution, links, clover, source, out):
    local_body(lambda spin, half: load_spin(solution, spin, half), links, clover, source, out)


def hops(local, links, received, comp, half):
    top, bottom = load_spin(local, comp, half), load_spin(local, 2 + comp, half)
    for mu, ahead, behind in received:
        hopped = link_times(links, mu, half, ahead(comp, half, mu, -1), False)
        top, bottom = accumulate(top, bottom, mu, comp, -1, hopped)
        top, bottom = accumulate(top, bottom, mu, comp, 1, behind(comp, half, mu, 1))
    return top, bottom


def from_halves(ref):
    return lambda comp, half, mu, sign: load_spin(ref, comp, half)


def from_source(ref):
    def load(comp, half, mu, sign):
        whole = source_spinor(ref)
        return half_spin(mu, comp, sign, whole(comp, half), whole(2 + comp, half))

    return load


def arrivals(*refs):
    return [
        (mu, from_halves(Pick(even, *after)), from_halves(Pick(even, *before)))
        for mu, even, after, before in neighbours(*refs)
    ]


def step_body(received, time_rank, space_rank, local, links, solution, *sends):
    for comp in range(2):
        for half in range(2):
            top, bottom = hops(local, links, received, comp, half)
            store_spin(solution, comp, half, top)
            store_spin(solution, 2 + comp, half, bottom)
            for mu, rank, inner, outer in (
                (3, time_rank, *sends[:2]),
                (2, space_rank, *sends[2:]),
            ):
                ahead = half_spin(mu, comp, -1, top, bottom)
                plus = half_spin(mu, comp, 1, top, bottom)
                behind = link_times(links, mu, half, plus, True)
                store_sends(inner, outer, is_even(rank), comp, half, behind, ahead)


def step_first_kernel(sizes, time_rank, space_rank, bits, local, links, ti, to, zi, zo,
                      solution, sti, sto, szi, szo, at, bt, az, bz):
    time, space = time_rank[0], space_rank[0]
    own = source_weight(bits, time)
    later = source_weight(bits, lax.rem(time + 1, sizes[0]))
    earlier = source_weight(bits, lax.rem(time + sizes[0] - 1, sizes[0]))
    blocks = neighbours(time_rank, space_rank, ti, to, zi, zo)
    for (mu, even, after, before), ahead, behind, up, down, crosses in (
        (blocks[0], at, bt, later, earlier, time == 0),
        (blocks[1], az, bz, own, own, space == 0),
    ):
        down = down * hop_factor(bits, mu, crosses)
        for half in range(2):
            vector = []
            for c in range(3):
                pair = []
                for p in range(2):
                    plane = (c * 2 + p) * 2 + half
                    next_block, last_block = (
                        jnp.where(even, *(ref[pl.ds(base + plane, 8, stride=12), :] for ref, base in sides))
                        for sides in (after, before)
                    )
                    ahead[plane] = next_block * up
                    pair.append(last_block * down)
                vector.append(tuple(pair))
            moved = link_times(PackedLinks(even, *before), mu, half, vector, True)
            store_spin(behind, 0, half, moved)
    received = ((3, from_source(at), from_source(bt)), (2, from_source(az), from_source(bz)))
    step_body(received, time_rank, space_rank, local, links, solution, sti, sto, szi, szo)


def step_kernel(time_rank, space_rank, local, links, ti, to, zi, zo, *outs):
    received = arrivals(time_rank, space_rank, ti, to, zi, zo)
    step_body(received, time_rank, space_rank, local, links, *outs)


def modes_kernel(modes, out):
    count = modes.shape[0] // 12
    out[...] = jnp.zeros(out.shape, out.dtype)
    for c in range(3):
        for half in range(2):
            real = modes[pl.ds(4 * c + half, count, stride=12), :]
            imag = modes[pl.ds(4 * c + 2 + half, count, stride=12), :]
            lanes = slice(half * LANES, half * LANES + LANES)
            for p, upper, lower in ((0, real, -imag), (1, imag, real)):
                for start, value in ((0, upper), (count, lower)):
                    high = value.astype(jnp.bfloat16)
                    low = (value - high.astype(F32)).astype(jnp.bfloat16)
                    out[2 * c + p, start : start + count, lanes] = high
                    out[2 * c + p, 128 + start : 128 + start + count, lanes] = low


def last_kernel(time_rank, space_rank, local, links, ti, to, zi, zo, modes, out, rows):
    received = arrivals(time_rank, space_rank, ti, to, zi, zo)
    for comp in range(2):
        for half in range(2):
            pair = hops(local, links, received, comp, half)
            for spin, value in zip((comp, 2 + comp), pair, strict=True):
                for c in range(3):
                    for p in range(2):
                        rows[2 * c + p, 8 * spin : 8 * spin + 8, half * LANES : half * LANES + LANES] = value[c][p]
    total = None
    for plane in range(6):
        value = rows[plane]
        high = value.astype(jnp.bfloat16)
        low = (value - high.astype(F32)).astype(jnp.bfloat16)
        product = lax.dot_general(
            jnp.concatenate([high, low], 0),
            modes[plane],
            (((1,), (1,)), ((), ())),
            preferred_element_type=F32,
        )
        total = product if total is None else total + product
    total = total[:32, :128] + (total[:32, 128:] + total[32:, :128])
    for spin in range(4):
        out[pl.ds(spin, 8, stride=4), :] = total[8 * spin : 8 * spin + 8, : out.shape[1]]


def sum_kernel(parts, copies):
    total = jnp.sum(parts[...], axis=0, keepdims=True)
    copies[...] = jnp.broadcast_to(total, copies.shape)


def correlate_kernel(place, gathered, partner, row, out, rows):
    size = rows.shape[1]
    for time in range(rows.shape[0]):
        rows[time : time + 1, :] = gathered[swapped(time) : swapped(time) + 1, :]
    mine = rows[pl.ds(place[0], 1), :]
    row[...] = mine
    onehot = (
        partner[...] == lax.broadcasted_iota(jnp.int32, (size, size), 0)
    ).astype(F32)
    contract = (((1,), (1,)), ((), ()))
    own = jnp.broadcast_to(mine, (8, size))
    weighted = lax.dot_general(
        own, onehot, contract, precision=lax.Precision.HIGHEST, preferred_element_type=F32
    )
    found = lax.dot_general(
        weighted, rows[...], contract, precision=lax.Precision.HIGHEST, preferred_element_type=F32
    )
    out[...] = found[:1]


def call(kernel, outs, flops, scalars, *args, scratch=()):
    vmem = pl.BlockSpec(memory_space=pltpu.VMEM)
    smem = pl.BlockSpec(memory_space=pltpu.SMEM)
    single = not isinstance(outs, (list, tuple))
    shapes = [outs] if single else list(outs)
    moved = 4 * sum(a.size for a in args) + 4 * sum(s.size for s in shapes)
    out = pl.pallas_call(
        kernel,
        out_shape=outs,
        in_specs=[smem] * len(scalars) + [vmem] * len(args),
        out_specs=vmem if single else [vmem] * len(shapes),
        scratch_shapes=scratch,
        compiler_params=pltpu.CompilerParams(vmem_limit_bytes=16 << 20),
        cost_estimate=pl.CostEstimate(flops=flops, bytes_accessed=moved, transcendentals=0),
    )(*scalars, *args)
    return out


def vectors(count):
    return jax.ShapeDtypeStruct((count, 8, LANES), F32)


def swapped(index):
    return index ^ ((index // 2) % 2)


def swap(axis, shift, place=lambda index: index):
    size = lax.axis_size(axis)
    pairs = [(place((i + shift) % size), place((i + 1 + shift) % size)) for i in range(0, size, 2)]
    return pairs + [(j, i) for i, j in pairs]


def exchange(t_inner, t_outer, z_inner, z_outer):
    pairs = [[i, i + 1] for i in range(0, lax.axis_size("space"), 2)]
    zi = lax.all_gather(z_inner, "space", axis_index_groups=pairs, tiled=True)
    zo = lax.ppermute(z_outer, "space", swap("space", 1))
    to = lax.ppermute(t_outer, "tm", swap("tm", 1, swapped))
    if t_inner is None:
        return to, zi, zo
    ti = lax.ppermute(t_inner, "tm", swap("tm", 0))
    return ti, to, zi, zo


def mesh_ranks():
    return tuple(lax.axis_index(name).astype(jnp.int32).reshape(1) for name in ("tm", "space"))


def partial_rows(noise_field, gauge_links, clover, eigvecs, dilution, boundary):
    count = eigvecs.shape[0]
    noise = noise_field.reshape(-1, LANES)
    links_in = gauge_links.reshape(-1, LANES)
    clover = clover.reshape(-1, LANES)
    modes_in = eigvecs.reshape(-1, LANES)
    place, space_rank = mesh_ranks()
    moved = (place[0] // 2) % 2 == 1
    ranks = (swapped(place), space_rank)
    sizes = (lax.axis_size("tm"), lax.axis_size("space"))
    bits = jnp.concatenate([boundary, dilution])

    def prepare(*refs):
        prepare_kernel(sizes, *refs)

    def step_first(*refs):
        step_first_kernel(sizes, *refs)

    cut = links_in.shape[0] // 2
    packed = jnp.concatenate([noise, links_in[cut:], links_in[:cut]])
    other = lax.ppermute(packed, "tm", swap("tm", 0))
    other_clover = lax.ppermute(clover, "tm", swap("tm", 0))
    block, pair = jnp.where(moved, other, packed), jnp.where(moved, packed, other)
    clover = jnp.where(moved, other_clover, clover)
    block_sent = block[: packed.shape[0] - cut]
    solution = None
    for iteration in range(ITERS):
        if iteration == 0:
            arrived = (pair, *exchange(None, block_sent, block_sent, block_sent))
        else:
            arrived = exchange(*sends)
        if iteration == 1:
            other_modes = lax.ppermute(modes_in, "tm", swap("tm", 0))
            modes = call(
                modes_kernel,
                jax.ShapeDtypeStruct((6, 256, 256), jnp.bfloat16),
                10**6,
                (),
                jnp.where(moved, other_modes, modes_in),
            )
        if iteration == 0:
            links, source = call(
                prepare,
                [jax.ShapeDtypeStruct(links_in.shape, F32), vectors(12)],
                10**6,
                (*ranks, bits),
                block,
            )
            local = call(local_first_kernel, vectors(48), 5 * 10**6, (), links, clover, source)
        else:
            local = call(local_kernel, vectors(48), 5 * 10**6, (), solution, links, clover, source)
        if iteration < ITERS - 1:
            first = iteration == 0
            solution, *sends = call(
                step_first if first else step_kernel,
                [vectors(48)] + [vectors(24)] * 4,
                3 * 10**6,
                (*ranks, bits) if first else ranks,
                local, links, *arrived,
                scratch=[pltpu.VMEM((12, 8, LANES), F32)] * 4 if first else (),
            )
        else:
            partial_sums = call(
                last_kernel,
                jax.ShapeDtypeStruct((32, 2 * count), F32),
                10**7,
                ranks,
                local, links, *arrived, modes,
                scratch=[pltpu.VMEM((6, 32, 256), F32)],
            )
    return partial_sums


def shards(noise_field, gauge_links, clover, eigvecs, partner, dilution, boundary):
    count = eigvecs.shape[0]
    partial_sums = partial_rows(
        noise_field, gauge_links, clover, eigvecs, dilution, boundary
    )
    both = jnp.concatenate([partner, partner + count]).reshape(1, 2 * count)
    both, partial_sums = lax.optimization_barrier((both, partial_sums))
    parts = lax.all_to_all(partial_sums, "space", 0, 0, tiled=True)
    times = lax.axis_size("tm")
    copies = call(
        sum_kernel, jax.ShapeDtypeStruct((times, 2 * count), F32), 10**4, (), parts
    )
    gathered = lax.all_to_all(copies, "tm", 0, 0, tiled=True)
    row, correlator = call(
        correlate_kernel,
        [jax.ShapeDtypeStruct((1, n), F32) for n in (2 * count, times)],
        10**5,
        mesh_ranks()[:1],
        gathered,
        both,
        scratch=[pltpu.VMEM((times, 2 * count), F32)],
    )
    return row.reshape(1, 1, 2 * count), correlator.reshape(1, 1, times)


def solution(mesh):
    return jax.shard_map(
        shards,
        mesh=mesh,
        in_specs=(
            P(None, "tm", "space", None, None),
            P(None, None, "tm", "space", None, None),
            P(None, None, "tm", "space", None, None),
            P(None, "tm", "space", None, None),
            P(),
            P(),
            P(),
        ),
        out_specs=(P("space", "tm", None), P("space", "tm", None)),
        check_vma=False,
    )
```

```python
import jax
import jax.numpy as jnp
from jax import lax
from jax.experimental import pallas as pl
from jax.experimental.pallas import tpu as pltpu
from jax.sharding import PartitionSpec as P

ITERS = 4
DILUTE = 4
SIDE = 16
LANES = 128
diag_term = 4.1
step_size = 0.2
F32 = jnp.float32

twist_table = (
    (((1, 0, -1), (0, 0, -1)), ((1, 0, 1), (0, 0, 1))),
    (((1, -1, 0), (0, 1, 0)), ((1, 1, 0), (0, -1, 0))),
    (((0, 0, -1), (1, 0, 1)), ((0, 0, 1), (1, 0, -1))),
    (((0, 1, 0), (1, 1, 0)), ((0, 1, 0), (1, 1, 0))),
)


def add_scaled(pair, sign, coef, other):
    real_coef, imag_coef = coef
    if imag_coef == 0:
        if sign * real_coef > 0:
            return (pair[0] + other[0], pair[1] + other[1])
        return (pair[0] - other[0], pair[1] - other[1])
    if sign * imag_coef > 0:
        return (pair[0] - other[1], pair[1] + other[0])
    return (pair[0] + other[1], pair[1] - other[0])


def row8(ref, row):
    if isinstance(ref, PackedLinks):
        return jnp.where(ref.first, *(row8(side, row + base + 24) for side, base in ref.sides))
    return ref[pl.ds(row, 8, stride=0), :]


class PackedLinks:
    def __init__(self, first, *sides):
        self.first, self.sides = first, sides


def link_times(links, mu, half, vector, adjoint):
    out = []
    for i in range(3):
        real, imag = None, None
        for k in range(3):
            row, col = (k, i) if adjoint else (i, k)
            base = ((mu * 3 + row) * 6 + 2 * col) * 2 + half
            mr, mi = row8(links, base), row8(links, base + 2)
            vr, vi = vector[k]
            if adjoint:
                r, m = mr * vr + mi * vi, mr * vi - mi * vr
            else:
                r, m = mr * vr - mi * vi, mr * vi + mi * vr
            real = r if real is None else real + r
            imag = m if imag is None else imag + m
        out.append((real, imag))
    return out


def spinor_at(spin, color, part, half):
    return ((spin * 3 + color) * 2 + part) * 2 + half


def load_spin(ref, spin, half):
    return [
        tuple(ref[spinor_at(spin, c, p, half)] for p in range(2)) for c in range(3)
    ]


def store_spin(ref, spin, half, value):
    for c in range(3):
        for p in range(2):
            ref[spinor_at(spin, c, p, half)] = value[c][p]


def half_spin(mu, comp, sign, upper, lower):
    _, real_coef, imag_coef = twist_table[mu][0][comp]
    return [
        add_scaled(upper[c], sign, (real_coef, imag_coef), lower[c]) for c in range(3)
    ]


def lower_target(mu, comp):
    for target in range(2):
        source, real_coef, imag_coef = twist_table[mu][1][target]
        if source == comp:
            return target, (real_coef, imag_coef)
    raise ValueError


def lower_source(mu, comp):
    return twist_table[mu][0][comp][0]


def accumulate(top, bottom, mu, comp, sign, hopped):
    _, coef = lower_target(mu, comp)
    top = [(top[c][0] + hopped[c][0], top[c][1] + hopped[c][1]) for c in range(3)]
    bottom = [add_scaled(bottom[c], sign, coef, hopped[c]) for c in range(3)]
    return top, bottom


def source_rows(shape):
    return lax.broadcasted_iota(jnp.int32, shape, 0)


def spin_mask(spin):
    return source_rows((8, LANES)) % 4 == spin


class Pick:
    def __init__(self, first, *sides):
        self.first, self.sides = first, sides

    def __getitem__(self, index):
        return jnp.where(self.first, *(ref[base + index] for ref, base in self.sides))


def neighbours(time_rank, space_rank, ti, to, zi, zo):
    half = zi.shape[0] // 2
    return (
        (3, is_even(time_rank), ((ti, 0), (to, 0)), ((to, 0), (ti, 0))),
        (2, is_even(space_rank), ((zi, half), (zo, 0)), ((zo, 0), (zi, 0))),
    )


def is_even(rank):
    return jnp.full((8, LANES), rank[0], jnp.int32) % 2 == 0


def store_sends(inner, outer, even, comp, half, behind, ahead):
    for c in range(3):
        for p in range(2):
            up, down = behind[c][p], ahead[c][p]
            inner[spinor_at(comp, c, p, half)] = jnp.where(even, up, down)
            outer[spinor_at(comp, c, p, half)] = jnp.where(even, down, up)


def source_weight(bits, time):
    row = source_rows((8, LANES))
    weight = jnp.zeros((8, LANES), F32)
    for j in range(8):
        on = jnp.where(time % DILUTE == bits[4 + j], step_size, 0.0)
        weight = jnp.where(row == j, on, weight)
    return weight


def hop_factor(bits, mu, crosses):
    phase = (1 - 2 * bits[mu]).astype(F32) * (0.5 * step_size)
    return jnp.where(crosses, phase, 0.5 * step_size)


def prepare_kernel(sizes, time_rank, space_rank, bits, packed, links, source):
    lane = lax.broadcasted_iota(jnp.int32, (8, LANES), 1)
    row = lax.broadcasted_iota(jnp.int32, (8, LANES), 0)
    at_x = hop_factor(bits, 0, lane % SIDE == SIDE - 1)
    at_y = hop_factor(bits, 1, (lane >= LANES - SIDE) & (row % 2 == 1))
    at_z = jnp.full((8, LANES), hop_factor(bits, 2, space_rank[0] == sizes[1] - 1))
    at_t = jnp.full((8, LANES), hop_factor(bits, 3, time_rank[0] == sizes[0] - 1))
    scales = (at_x, at_y, at_z, at_t)
    for block in range(18):
        first, last = (block * 8) // 36, (block * 8 + 7) // 36
        scale = scales[first]
        if last != first:
            scale = jnp.where(row + block * 8 >= last * 36, scales[last], scale)
        from_row = 8 * block + (168 if block < 9 else 24)
        links[block * 8 : block * 8 + 8, :] = packed[from_row : from_row + 8, :] * scale
    weight = source_weight(bits, time_rank[0])
    for plane in range(12):
        source[plane] = packed[pl.ds(plane, 8, stride=12), :] * weight


def shift_x(value, forward):
    lane = lax.broadcasted_iota(jnp.int32, (8, LANES), 1) % SIDE
    if forward:
        return jnp.where(
            lane == SIDE - 1,
            pltpu.roll(value, SIDE - 1, 1),
            pltpu.roll(value, LANES - 1, 1),
        )
    return jnp.where(
        lane == 0, pltpu.roll(value, LANES - SIDE + 1, 1), pltpu.roll(value, 1, 1)
    )


def shift_y(low, high, forward):
    lane = lax.broadcasted_iota(jnp.int32, (8, LANES), 1)
    if forward:
        a, b = pltpu.roll(low, LANES - SIDE, 1), pltpu.roll(high, LANES - SIDE, 1)
        keep = lane < LANES - SIDE
    else:
        a, b = pltpu.roll(low, SIDE, 1), pltpu.roll(high, SIDE, 1)
        keep = lane >= SIDE
    return jnp.where(keep, a, b), jnp.where(keep, b, a)


def shift_plane(mu, pair_of_halves, forward):
    moved = ([], [])
    for c in range(3):
        parts = ([], [])
        for p in range(2):
            low, high = pair_of_halves[0][c][p], pair_of_halves[1][c][p]
            if mu == 0:
                low, high = shift_x(low, forward), shift_x(high, forward)
            else:
                low, high = shift_y(low, high, forward)
            parts[0].append(low)
            parts[1].append(high)
        moved[0].append(tuple(parts[0]))
        moved[1].append(tuple(parts[1]))
    return moved


def local_body(load, links, clover, source, out):
    for chiral in range(2):
        for half in range(2):
            vector = load(2 * chiral, half) + load(2 * chiral + 1, half)
            for a in range(6):
                real, imag = None, None
                for b in range(6):
                    base = ((chiral * 6 + a) * 12 + 2 * b) * 2 + half
                    mr, mi = row8(clover, base), row8(clover, base + 2)
                    vr, vi = vector[b]
                    r, m = mr * vr - mi * vi, mr * vi + mi * vr
                    real = r if real is None else real + r
                    imag = m if imag is None else imag + m
                spin, color = 2 * chiral + a // 3, a % 3
                here = spin_mask(spin)
                keep = 1.0 - step_size * diag_term
                for p, total in ((0, real), (1, imag)):
                    value = keep * vector[a][p] - step_size * total
                    value = value + jnp.where(here, source[(color * 2 + p) * 2 + half], 0.0)
                    out[spinor_at(spin, color, p, half)] = value
    for comp in range(2):
        low_spin = 2 + lower_source(0, comp)
        upper = [load(comp, half) for half in range(2)]
        lower = [load(low_spin, half) for half in range(2)]
        top = [load_spin(out, comp, half) for half in range(2)]
        bottom = [load_spin(out, low_spin, half) for half in range(2)]
        for mu in range(2):
            ahead = [half_spin(mu, comp, -1, upper[h], lower[h]) for h in range(2)]
            ahead = shift_plane(mu, ahead, True)
            for h in range(2):
                hopped = link_times(links, mu, h, ahead[h], False)
                top[h], bottom[h] = accumulate(top[h], bottom[h], mu, comp, -1, hopped)
            behind = [
                link_times(links, mu, h, half_spin(mu, comp, 1, upper[h], lower[h]), True)
                for h in range(2)
            ]
            behind = shift_plane(mu, behind, False)
            for h in range(2):
                top[h], bottom[h] = accumulate(top[h], bottom[h], mu, comp, 1, behind[h])
        for h in range(2):
            store_spin(out, comp, h, top[h])
            store_spin(out, low_spin, h, bottom[h])


def source_spinor(source):
    def load(spin, half):
        here = spin_mask(spin)
        return [
            tuple(jnp.where(here, source[(c * 2 + p) * 2 + half], 0.0) for p in range(2))
            for c in range(3)
        ]

    return load


def local_first_kernel(links, clover, source, out):
    local_body(source_spinor(source), links, clover, source, out)


def local_kernel(solution, links, clover, source, out):
    local_body(lambda spin, half: load_spin(solution, spin, half), links, clover, source, out)


def hops(local, links, received, comp, half):
    top, bottom = load_spin(local, comp, half), load_spin(local, 2 + comp, half)
    for mu, ahead, behind in received:
        hopped = link_times(links, mu, half, ahead(comp, half, mu, -1), False)
        top, bottom = accumulate(top, bottom, mu, comp, -1, hopped)
        top, bottom = accumulate(top, bottom, mu, comp, 1, behind(comp, half, mu, 1))
    return top, bottom


def from_halves(ref):
    return lambda comp, half, mu, sign: load_spin(ref, comp, half)


def from_source(ref):
    def load(comp, half, mu, sign):
        whole = source_spinor(ref)
        return half_spin(mu, comp, sign, whole(comp, half), whole(2 + comp, half))

    return load


def arrivals(*refs):
    return [
        (mu, from_halves(Pick(even, *after)), from_halves(Pick(even, *before)))
        for mu, even, after, before in neighbours(*refs)
    ]


def step_body(received, time_rank, space_rank, local, links, carried, solution, *sends):
    if carried is not None:
        sends[0][24:] = carried[...]
    for comp in range(2):
        for half in range(2):
            top, bottom = hops(local, links, received, comp, half)
            store_spin(solution, comp, half, top)
            store_spin(solution, 2 + comp, half, bottom)
            for mu, rank, inner, outer in (
                (3, time_rank, *sends[:2]),
                (2, space_rank, *sends[2:]),
            ):
                ahead = half_spin(mu, comp, -1, top, bottom)
                plus = half_spin(mu, comp, 1, top, bottom)
                behind = link_times(links, mu, half, plus, True)
                store_sends(inner, outer, is_even(rank), comp, half, behind, ahead)


def step_first_kernel(sizes, time_rank, space_rank, bits, local, links, ti, to, zi, zo,
                      carried, solution, sti, sto, szi, szo, at, bt, az, bz):
    time, space = time_rank[0], space_rank[0]
    own = source_weight(bits, time)
    later = source_weight(bits, lax.rem(time + 1, sizes[0]))
    earlier = source_weight(bits, lax.rem(time + sizes[0] - 1, sizes[0]))
    blocks = neighbours(time_rank, space_rank, ti, to, zi, zo)
    for (mu, even, after, before), ahead, behind, up, down, crosses in (
        (blocks[0], at, bt, later, earlier, time == 0),
        (blocks[1], az, bz, own, own, space == 0),
    ):
        down = down * hop_factor(bits, mu, crosses)
        for half in range(2):
            vector = []
            for c in range(3):
                pair = []
                for p in range(2):
                    plane = (c * 2 + p) * 2 + half
                    next_block, last_block = (
                        jnp.where(even, *(ref[pl.ds(base + plane, 8, stride=12), :] for ref, base in sides))
                        for sides in (after, before)
                    )
                    ahead[plane] = next_block * up
                    pair.append(last_block * down)
                vector.append(tuple(pair))
            moved = link_times(PackedLinks(even, *before), mu, half, vector, True)
            store_spin(behind, 0, half, moved)
    received = ((3, from_source(at), from_source(bt)), (2, from_source(az), from_source(bz)))
    step_body(received, time_rank, space_rank, local, links, carried, solution, sti, sto, szi, szo)


def step_carry_kernel(time_rank, space_rank, local, links, ti, to, zi, zo, *refs):
    received = arrivals(time_rank, space_rank, ti, to, zi, zo)
    step_body(received, time_rank, space_rank, local, links, *refs)


def step_kernel(time_rank, space_rank, local, links, ti, to, zi, zo, *outs):
    received = arrivals(time_rank, space_rank, ti, to, zi, zo)
    step_body(received, time_rank, space_rank, local, links, None, *outs)


def modes_kernel(modes, out):
    count = modes.shape[0] // 12
    out[...] = jnp.zeros(out.shape, out.dtype)
    for c in range(3):
        for half in range(2):
            real = modes[pl.ds(4 * c + half, count, stride=12), :]
            imag = modes[pl.ds(4 * c + 2 + half, count, stride=12), :]
            lanes = slice(half * LANES, half * LANES + LANES)
            for p, upper, lower in ((0, real, -imag), (1, imag, real)):
                for start, value in ((0, upper), (count, lower)):
                    high = value.astype(jnp.bfloat16)
                    low = (value - high.astype(F32)).astype(jnp.bfloat16)
                    out[2 * c + p, start : start + count, lanes] = high
                    out[2 * c + p, 128 + start : 128 + start + count, lanes] = low


def last_kernel(time_rank, space_rank, local, links, ti, to, zi, zo, modes, out, rows):
    received = arrivals(time_rank, space_rank, ti, to, zi, zo)
    for comp in range(2):
        for half in range(2):
            pair = hops(local, links, received, comp, half)
            for spin, value in zip((comp, 2 + comp), pair, strict=True):
                for c in range(3):
                    for p in range(2):
                        rows[2 * c + p, 8 * spin : 8 * spin + 8, half * LANES : half * LANES + LANES] = value[c][p]
    total = None
    for plane in range(6):
        value = rows[plane]
        high = value.astype(jnp.bfloat16)
        low = (value - high.astype(F32)).astype(jnp.bfloat16)
        product = lax.dot_general(
            jnp.concatenate([high, low], 0),
            modes[plane],
            (((1,), (1,)), ((), ())),
            preferred_element_type=F32,
        )
        total = product if total is None else total + product
    total = total[:32, :128] + (total[:32, 128:] + total[32:, :128])
    for spin in range(4):
        out[pl.ds(spin, 8, stride=4), :] = total[8 * spin : 8 * spin + 8, : out.shape[1]]


def sum_kernel(parts, copies):
    total = jnp.sum(parts[...], axis=0, keepdims=True)
    copies[...] = jnp.broadcast_to(total, copies.shape)


def correlate_kernel(place, gathered, partner, row, out, rows):
    size = rows.shape[1]
    for time in range(rows.shape[0]):
        rows[time : time + 1, :] = gathered[swapped(time) : swapped(time) + 1, :]
    mine = rows[pl.ds(place[0], 1), :]
    row[...] = mine
    onehot = (
        partner[...] == lax.broadcasted_iota(jnp.int32, (size, size), 0)
    ).astype(F32)
    contract = (((1,), (1,)), ((), ()))
    own = jnp.broadcast_to(mine, (8, size))
    weighted = lax.dot_general(
        own, onehot, contract, precision=lax.Precision.HIGHEST, preferred_element_type=F32
    )
    found = lax.dot_general(
        weighted, rows[...], contract, precision=lax.Precision.HIGHEST, preferred_element_type=F32
    )
    out[...] = found[:1]


def call(kernel, outs, flops, scalars, *args, scratch=()):
    vmem = pl.BlockSpec(memory_space=pltpu.VMEM)
    smem = pl.BlockSpec(memory_space=pltpu.SMEM)
    single = not isinstance(outs, (list, tuple))
    shapes = [outs] if single else list(outs)
    moved = 4 * sum(a.size for a in args) + 4 * sum(s.size for s in shapes)
    out = pl.pallas_call(
        kernel,
        out_shape=outs,
        in_specs=[smem] * len(scalars) + [vmem] * len(args),
        out_specs=vmem if single else [vmem] * len(shapes),
        scratch_shapes=scratch,
        compiler_params=pltpu.CompilerParams(vmem_limit_bytes=16 << 20),
        cost_estimate=pl.CostEstimate(flops=flops, bytes_accessed=moved, transcendentals=0),
    )(*scalars, *args)
    return out


def vectors(count):
    return jax.ShapeDtypeStruct((count, 8, LANES), F32)


def swapped(index):
    return index ^ ((index // 2) % 2)


def swap(axis, shift, place=lambda index: index):
    size = lax.axis_size(axis)
    pairs = [(place((i + shift) % size), place((i + 1 + shift) % size)) for i in range(0, size, 2)]
    return pairs + [(j, i) for i, j in pairs]


def exchange(t_inner, t_outer, z_inner, z_outer):
    pairs = [[i, i + 1] for i in range(0, lax.axis_size("space"), 2)]
    zi = lax.all_gather(z_inner, "space", axis_index_groups=pairs, tiled=True)
    zo = lax.ppermute(z_outer, "space", swap("space", 1))
    to = lax.ppermute(t_outer, "tm", swap("tm", 1, swapped))
    if t_inner is None:
        return to, zi, zo
    ti = lax.ppermute(t_inner, "tm", swap("tm", 0))
    return ti, to, zi, zo


def mesh_ranks():
    return tuple(lax.axis_index(name).astype(jnp.int32).reshape(1) for name in ("tm", "space"))


def partial_rows(noise_field, gauge_links, clover, eigvecs, dilution, boundary):
    count = eigvecs.shape[0]
    noise = noise_field.reshape(-1, LANES)
    links_in = gauge_links.reshape(-1, LANES)
    clover = clover.reshape(-1, LANES)
    modes_in = eigvecs.reshape(-1, LANES)
    place, space_rank = mesh_ranks()
    moved = (place[0] // 2) % 2 == 1
    ranks = (swapped(place), space_rank)
    sizes = (lax.axis_size("tm"), lax.axis_size("space"))
    bits = jnp.concatenate([boundary, dilution])

    def prepare(*refs):
        prepare_kernel(sizes, *refs)

    def step_first(*refs):
        step_first_kernel(sizes, *refs)

    cut = links_in.shape[0] // 2
    packed = jnp.concatenate([noise, links_in[cut:], links_in[:cut]])
    other = lax.ppermute(packed, "tm", swap("tm", 0))
    other_clover = lax.ppermute(clover, "tm", swap("tm", 0))
    block, pair = jnp.where(moved, other, packed), jnp.where(moved, packed, other)
    clover = jnp.where(moved, other_clover, clover)
    block_sent = block[: packed.shape[0] - cut]
    solution, other_modes = None, []
    modes_halves = modes_in.reshape(2, -1, 8, LANES)
    for iteration in range(ITERS):
        if iteration == 0:
            arrived = (pair, *exchange(None, block_sent, block_sent, block_sent))
        else:
            arrived = exchange(*sends)
        if iteration in (1, 2):
            other_modes.append(arrived[0][24:])
        if iteration == 2:
            modes = call(
                modes_kernel,
                jax.ShapeDtypeStruct((6, 256, 256), jnp.bfloat16),
                10**6,
                (),
                jnp.where(moved, jnp.concatenate(other_modes).reshape(modes_in.shape), modes_in),
            )
        if iteration == 0:
            links, source = call(
                prepare,
                [jax.ShapeDtypeStruct(links_in.shape, F32), vectors(12)],
                10**6,
                (*ranks, bits),
                block,
            )
            local = call(local_first_kernel, vectors(48), 5 * 10**6, (), links, clover, source)
        else:
            local = call(local_kernel, vectors(48), 5 * 10**6, (), solution, links, clover, source)
        if iteration < ITERS - 1:
            first = iteration == 0
            carried = (modes_halves[iteration],) if iteration < 2 else ()
            body = (step_first, step_carry_kernel, step_kernel)[iteration]
            inner = 24 + sum(half.shape[0] for half in carried)
            solution, *sends = call(
                body,
                [vectors(48), vectors(inner)] + [vectors(24)] * 3,
                3 * 10**6,
                (*ranks, bits) if first else ranks,
                local, links, *arrived, *carried,
                scratch=[pltpu.VMEM((12, 8, LANES), F32)] * 4 if first else (),
            )
        else:
            partial_sums = call(
                last_kernel,
                jax.ShapeDtypeStruct((32, 2 * count), F32),
                10**7,
                ranks,
                local, links, *arrived, modes,
                scratch=[pltpu.VMEM((6, 32, 256), F32)],
            )
    return partial_sums


def shards(noise_field, gauge_links, clover, eigvecs, partner, dilution, boundary):
    count = eigvecs.shape[0]
    partial_sums = partial_rows(
        noise_field, gauge_links, clover, eigvecs, dilution, boundary
    )
    both = jnp.concatenate([partner, partner + count]).reshape(1, 2 * count)
    both, partial_sums = lax.optimization_barrier((both, partial_sums))
    parts = lax.all_to_all(partial_sums, "space", 0, 0, tiled=True)
    times = lax.axis_size("tm")
    copies = call(
        sum_kernel, jax.ShapeDtypeStruct((times, 2 * count), F32), 10**4, (), parts
    )
    gathered = lax.all_to_all(copies, "tm", 0, 0, tiled=True)
    row, correlator = call(
        correlate_kernel,
        [jax.ShapeDtypeStruct((1, n), F32) for n in (2 * count, times)],
        10**5,
        mesh_ranks()[:1],
        gathered,
        both,
        scratch=[pltpu.VMEM((times, 2 * count), F32)],
    )
    return row.reshape(1, 1, 2 * count), correlator.reshape(1, 1, times)


def solution(mesh):
    return jax.shard_map(
        shards,
        mesh=mesh,
        in_specs=(
            P(None, "tm", "space", None, None),
            P(None, None, "tm", "space", None, None),
            P(None, None, "tm", "space", None, None),
            P(None, "tm", "space", None, None),
            P(),
            P(),
            P(),
        ),
        out_specs=(P("space", "tm", None), P("space", "tm", None)),
        check_vma=False,
    )
```

```python
import jax
import jax.numpy as jnp
from jax import lax
from jax.experimental import pallas as pl
from jax.experimental.pallas import tpu as pltpu
from jax.sharding import PartitionSpec as P

ITERS = 4
DILUTE = 4
SIDE = 16
LANES = 128
diag_term = 4.1
step_size = 0.2
F32 = jnp.float32

twist_table = (
    (((1, 0, -1), (0, 0, -1)), ((1, 0, 1), (0, 0, 1))),
    (((1, -1, 0), (0, 1, 0)), ((1, 1, 0), (0, -1, 0))),
    (((0, 0, -1), (1, 0, 1)), ((0, 0, 1), (1, 0, -1))),
    (((0, 1, 0), (1, 1, 0)), ((0, 1, 0), (1, 1, 0))),
)


def add_scaled(pair, sign, coef, other):
    real_coef, imag_coef = coef
    if imag_coef == 0:
        if sign * real_coef > 0:
            return (pair[0] + other[0], pair[1] + other[1])
        return (pair[0] - other[0], pair[1] - other[1])
    if sign * imag_coef > 0:
        return (pair[0] - other[1], pair[1] + other[0])
    return (pair[0] + other[1], pair[1] - other[0])


def row8(ref, row):
    if isinstance(ref, PackedLinks):
        return jnp.where(ref.first, *(row8(side, row + base + 24) for side, base in ref.sides))
    return ref[pl.ds(row, 8, stride=0), :]


class PackedLinks:
    def __init__(self, first, *sides):
        self.first, self.sides = first, sides


def link_times(links, mu, half, vector, adjoint):
    out = []
    for i in range(3):
        real, imag = None, None
        for k in range(3):
            row, col = (k, i) if adjoint else (i, k)
            base = ((mu * 3 + row) * 6 + 2 * col) * 2 + half
            mr, mi = row8(links, base), row8(links, base + 2)
            vr, vi = vector[k]
            if adjoint:
                r, m = mr * vr + mi * vi, mr * vi - mi * vr
            else:
                r, m = mr * vr - mi * vi, mr * vi + mi * vr
            real = r if real is None else real + r
            imag = m if imag is None else imag + m
        out.append((real, imag))
    return out


def spinor_at(spin, color, part, half):
    return ((spin * 3 + color) * 2 + part) * 2 + half


def load_spin(ref, spin, half):
    return [
        tuple(ref[spinor_at(spin, c, p, half)] for p in range(2)) for c in range(3)
    ]


def store_spin(ref, spin, half, value):
    for c in range(3):
        for p in range(2):
            ref[spinor_at(spin, c, p, half)] = value[c][p]


def half_spin(mu, comp, sign, upper, lower):
    _, real_coef, imag_coef = twist_table[mu][0][comp]
    return [
        add_scaled(upper[c], sign, (real_coef, imag_coef), lower[c]) for c in range(3)
    ]


def lower_target(mu, comp):
    for target in range(2):
        source, real_coef, imag_coef = twist_table[mu][1][target]
        if source == comp:
            return target, (real_coef, imag_coef)
    raise ValueError


def lower_source(mu, comp):
    return twist_table[mu][0][comp][0]


def accumulate(top, bottom, mu, comp, sign, hopped):
    _, coef = lower_target(mu, comp)
    top = [(top[c][0] + hopped[c][0], top[c][1] + hopped[c][1]) for c in range(3)]
    bottom = [add_scaled(bottom[c], sign, coef, hopped[c]) for c in range(3)]
    return top, bottom


def source_rows(shape):
    return lax.broadcasted_iota(jnp.int32, shape, 0)


def spin_mask(spin):
    return source_rows((8, LANES)) % 4 == spin


class Pick:
    def __init__(self, first, *sides):
        self.first, self.sides = first, sides

    def __getitem__(self, index):
        return jnp.where(self.first, *(ref[base + index] for ref, base in self.sides))


def neighbours(time_rank, space_rank, ti, to, zi, zo):
    half = zi.shape[0] // 2
    return (
        (3, is_even(time_rank), ((ti, 0), (to, 0)), ((to, 0), (ti, 0))),
        (2, is_even(space_rank), ((zi, half), (zo, 0)), ((zo, 0), (zi, 0))),
    )


def is_even(rank):
    return jnp.full((8, LANES), rank[0], jnp.int32) % 2 == 0


def store_sends(inner, outer, even, comp, half, behind, ahead):
    for c in range(3):
        for p in range(2):
            up, down = behind[c][p], ahead[c][p]
            inner[spinor_at(comp, c, p, half)] = jnp.where(even, up, down)
            outer[spinor_at(comp, c, p, half)] = jnp.where(even, down, up)


def source_weight(bits, time):
    row = source_rows((8, LANES))
    weight = jnp.zeros((8, LANES), F32)
    for j in range(8):
        on = jnp.where(time % DILUTE == bits[4 + j], step_size, 0.0)
        weight = jnp.where(row == j, on, weight)
    return weight


def hop_factor(bits, mu, crosses):
    phase = (1 - 2 * bits[mu]).astype(F32) * (0.5 * step_size)
    return jnp.where(crosses, phase, 0.5 * step_size)


def prepare_kernel(sizes, time_rank, space_rank, bits, noise, links_in, links, source):
    lane = lax.broadcasted_iota(jnp.int32, (8, LANES), 1)
    row = lax.broadcasted_iota(jnp.int32, (8, LANES), 0)
    at_x = hop_factor(bits, 0, lane % SIDE == SIDE - 1)
    at_y = hop_factor(bits, 1, (lane >= LANES - SIDE) & (row % 2 == 1))
    at_z = jnp.full((8, LANES), hop_factor(bits, 2, space_rank[0] == sizes[1] - 1))
    at_t = jnp.full((8, LANES), hop_factor(bits, 3, time_rank[0] == sizes[0] - 1))
    scales = (at_x, at_y, at_z, at_t)
    for block in range(18):
        first, last = (block * 8) // 36, (block * 8 + 7) // 36
        scale = scales[first]
        if last != first:
            scale = jnp.where(row + block * 8 >= last * 36, scales[last], scale)
        links[block * 8 : block * 8 + 8, :] = links_in[block * 8 : block * 8 + 8, :] * scale
    weight = source_weight(bits, time_rank[0])
    for plane in range(12):
        source[plane] = noise[pl.ds(plane, 8, stride=12), :] * weight


def shift_x(value, forward):
    lane = lax.broadcasted_iota(jnp.int32, (8, LANES), 1) % SIDE
    if forward:
        return jnp.where(
            lane == SIDE - 1,
            pltpu.roll(value, SIDE - 1, 1),
            pltpu.roll(value, LANES - 1, 1),
        )
    return jnp.where(
        lane == 0, pltpu.roll(value, LANES - SIDE + 1, 1), pltpu.roll(value, 1, 1)
    )


def shift_y(low, high, forward):
    lane = lax.broadcasted_iota(jnp.int32, (8, LANES), 1)
    if forward:
        a, b = pltpu.roll(low, LANES - SIDE, 1), pltpu.roll(high, LANES - SIDE, 1)
        keep = lane < LANES - SIDE
    else:
        a, b = pltpu.roll(low, SIDE, 1), pltpu.roll(high, SIDE, 1)
        keep = lane >= SIDE
    return jnp.where(keep, a, b), jnp.where(keep, b, a)


def shift_plane(mu, pair_of_halves, forward):
    moved = ([], [])
    for c in range(3):
        parts = ([], [])
        for p in range(2):
            low, high = pair_of_halves[0][c][p], pair_of_halves[1][c][p]
            if mu == 0:
                low, high = shift_x(low, forward), shift_x(high, forward)
            else:
                low, high = shift_y(low, high, forward)
            parts[0].append(low)
            parts[1].append(high)
        moved[0].append(tuple(parts[0]))
        moved[1].append(tuple(parts[1]))
    return moved


def local_body(load, links, clover, source, out):
    for chiral in range(2):
        for half in range(2):
            vector = load(2 * chiral, half) + load(2 * chiral + 1, half)
            for a in range(6):
                real, imag = None, None
                for b in range(6):
                    base = ((chiral * 6 + a) * 12 + 2 * b) * 2 + half
                    mr, mi = row8(clover, base), row8(clover, base + 2)
                    vr, vi = vector[b]
                    r, m = mr * vr - mi * vi, mr * vi + mi * vr
                    real = r if real is None else real + r
                    imag = m if imag is None else imag + m
                spin, color = 2 * chiral + a // 3, a % 3
                here = spin_mask(spin)
                keep = 1.0 - step_size * diag_term
                for p, total in ((0, real), (1, imag)):
                    value = keep * vector[a][p] - step_size * total
                    value = value + jnp.where(here, source[(color * 2 + p) * 2 + half], 0.0)
                    out[spinor_at(spin, color, p, half)] = value
    for comp in range(2):
        low_spin = 2 + lower_source(0, comp)
        upper = [load(comp, half) for half in range(2)]
        lower = [load(low_spin, half) for half in range(2)]
        top = [load_spin(out, comp, half) for half in range(2)]
        bottom = [load_spin(out, low_spin, half) for half in range(2)]
        for mu in range(2):
            ahead = [half_spin(mu, comp, -1, upper[h], lower[h]) for h in range(2)]
            ahead = shift_plane(mu, ahead, True)
            for h in range(2):
                hopped = link_times(links, mu, h, ahead[h], False)
                top[h], bottom[h] = accumulate(top[h], bottom[h], mu, comp, -1, hopped)
            behind = [
                link_times(links, mu, h, half_spin(mu, comp, 1, upper[h], lower[h]), True)
                for h in range(2)
            ]
            behind = shift_plane(mu, behind, False)
            for h in range(2):
                top[h], bottom[h] = accumulate(top[h], bottom[h], mu, comp, 1, behind[h])
        for h in range(2):
            store_spin(out, comp, h, top[h])
            store_spin(out, low_spin, h, bottom[h])


def source_spinor(source):
    def load(spin, half):
        here = spin_mask(spin)
        return [
            tuple(jnp.where(here, source[(c * 2 + p) * 2 + half], 0.0) for p in range(2))
            for c in range(3)
        ]

    return load


def local_first_kernel(links, clover, source, out):
    local_body(source_spinor(source), links, clover, source, out)


def local_kernel(solution, links, clover, source, out):
    local_body(lambda spin, half: load_spin(solution, spin, half), links, clover, source, out)


def hops(local, links, received, comp, half):
    top, bottom = load_spin(local, comp, half), load_spin(local, 2 + comp, half)
    for mu, ahead, behind in received:
        hopped = link_times(links, mu, half, ahead(comp, half, mu, -1), False)
        top, bottom = accumulate(top, bottom, mu, comp, -1, hopped)
        top, bottom = accumulate(top, bottom, mu, comp, 1, behind(comp, half, mu, 1))
    return top, bottom


def from_halves(ref):
    return lambda comp, half, mu, sign: load_spin(ref, comp, half)


def from_source(ref):
    def load(comp, half, mu, sign):
        whole = source_spinor(ref)
        return half_spin(mu, comp, sign, whole(comp, half), whole(2 + comp, half))

    return load


def arrivals(*refs):
    return [
        (mu, from_halves(Pick(even, *after)), from_halves(Pick(even, *before)))
        for mu, even, after, before in neighbours(*refs)
    ]


def step_body(received, time_rank, space_rank, local, links, solution, *sends):
    for comp in range(2):
        for half in range(2):
            top, bottom = hops(local, links, received, comp, half)
            store_spin(solution, comp, half, top)
            store_spin(solution, 2 + comp, half, bottom)
            for mu, rank, inner, outer in (
                (3, time_rank, *sends[:2]),
                (2, space_rank, *sends[2:]),
            ):
                ahead = half_spin(mu, comp, -1, top, bottom)
                plus = half_spin(mu, comp, 1, top, bottom)
                behind = link_times(links, mu, half, plus, True)
                store_sends(inner, outer, is_even(rank), comp, half, behind, ahead)


def step_first_kernel(sizes, time_rank, space_rank, bits, local, links, ti, to, zi, zo,
                      solution, sti, sto, szi, szo, at, bt, az, bz):
    time, space = time_rank[0], space_rank[0]
    own = source_weight(bits, time)
    later = source_weight(bits, lax.rem(time + 1, sizes[0]))
    earlier = source_weight(bits, lax.rem(time + sizes[0] - 1, sizes[0]))
    blocks = neighbours(time_rank, space_rank, ti, to, zi, zo)
    for (mu, even, after, before), ahead, behind, up, down, crosses in (
        (blocks[0], at, bt, later, earlier, time == 0),
        (blocks[1], az, bz, own, own, space == 0),
    ):
        down = down * hop_factor(bits, mu, crosses)
        for half in range(2):
            vector = []
            for c in range(3):
                pair = []
                for p in range(2):
                    plane = (c * 2 + p) * 2 + half
                    next_block, last_block = (
                        jnp.where(even, *(ref[pl.ds(base + plane, 8, stride=12), :] for ref, base in sides))
                        for sides in (after, before)
                    )
                    ahead[plane] = next_block * up
                    pair.append(last_block * down)
                vector.append(tuple(pair))
            moved = link_times(PackedLinks(even, *before), mu, half, vector, True)
            store_spin(behind, 0, half, moved)
    received = ((3, from_source(at), from_source(bt)), (2, from_source(az), from_source(bz)))
    step_body(received, time_rank, space_rank, local, links, solution, sti, sto, szi, szo)


def step_kernel(time_rank, space_rank, local, links, ti, to, zi, zo, *outs):
    received = arrivals(time_rank, space_rank, ti, to, zi, zo)
    step_body(received, time_rank, space_rank, local, links, *outs)


def modes_kernel(modes, out):
    count = modes.shape[0] // 12
    out[...] = jnp.zeros(out.shape, out.dtype)
    for c in range(3):
        for half in range(2):
            real = modes[pl.ds(4 * c + half, count, stride=12), :]
            imag = modes[pl.ds(4 * c + 2 + half, count, stride=12), :]
            lanes = slice(half * LANES, half * LANES + LANES)
            for p, upper, lower in ((0, real, -imag), (1, imag, real)):
                for start, value in ((0, upper), (count, lower)):
                    high = value.astype(jnp.bfloat16)
                    low = (value - high.astype(F32)).astype(jnp.bfloat16)
                    out[2 * c + p, start : start + count, lanes] = high
                    out[2 * c + p, 128 + start : 128 + start + count, lanes] = low


def last_kernel(time_rank, space_rank, local, links, ti, to, zi, zo, modes, out, rows):
    received = arrivals(time_rank, space_rank, ti, to, zi, zo)
    for comp in range(2):
        for half in range(2):
            pair = hops(local, links, received, comp, half)
            for spin, value in zip((comp, 2 + comp), pair, strict=True):
                for c in range(3):
                    for p in range(2):
                        rows[2 * c + p, 8 * spin : 8 * spin + 8, half * LANES : half * LANES + LANES] = value[c][p]
    total = None
    for plane in range(6):
        value = rows[plane]
        high = value.astype(jnp.bfloat16)
        low = (value - high.astype(F32)).astype(jnp.bfloat16)
        product = lax.dot_general(
            jnp.concatenate([high, low], 0),
            modes[plane],
            (((1,), (1,)), ((), ())),
            preferred_element_type=F32,
        )
        total = product if total is None else total + product
    total = total[:32, :128] + (total[:32, 128:] + total[32:, :128])
    for spin in range(4):
        out[pl.ds(spin, 8, stride=4), :] = total[8 * spin : 8 * spin + 8, : out.shape[1]]


def sum_kernel(parts, copies):
    total = jnp.sum(parts[...], axis=0, keepdims=True)
    copies[...] = jnp.broadcast_to(total, copies.shape)


def correlate_kernel(time_rank, rows, partner, row, out):
    size = rows.shape[1]
    mine = rows[pl.ds(time_rank[0], 1), :]
    row[...] = mine
    onehot = (
        partner[...] == lax.broadcasted_iota(jnp.int32, (size, size), 0)
    ).astype(F32)
    contract = (((1,), (1,)), ((), ()))
    own = jnp.broadcast_to(mine, (8, size))
    weighted = lax.dot_general(
        own, onehot, contract, precision=lax.Precision.HIGHEST, preferred_element_type=F32
    )
    found = lax.dot_general(
        weighted, rows[...], contract, precision=lax.Precision.HIGHEST, preferred_element_type=F32
    )
    out[...] = found[:1]


def call(kernel, outs, flops, scalars, *args, scratch=()):
    vmem = pl.BlockSpec(memory_space=pltpu.VMEM)
    smem = pl.BlockSpec(memory_space=pltpu.SMEM)
    single = not isinstance(outs, (list, tuple))
    shapes = [outs] if single else list(outs)
    moved = 4 * sum(a.size for a in args) + 4 * sum(s.size for s in shapes)
    out = pl.pallas_call(
        kernel,
        out_shape=outs,
        in_specs=[smem] * len(scalars) + [vmem] * len(args),
        out_specs=vmem if single else [vmem] * len(shapes),
        scratch_shapes=scratch,
        compiler_params=pltpu.CompilerParams(vmem_limit_bytes=16 << 20),
        cost_estimate=pl.CostEstimate(flops=flops, bytes_accessed=moved, transcendentals=0),
    )(*scalars, *args)
    return out


def vectors(count):
    return jax.ShapeDtypeStruct((count, 8, LANES), F32)


def exchange(t_inner, t_outer, z_inner, z_outer):
    def swap(axis, shift):
        size = lax.axis_size(axis)
        pairs = [((i + shift) % size, (i + 1 + shift) % size) for i in range(0, size, 2)]
        return pairs + [(j, i) for i, j in pairs]

    pairs = [[i, i + 1] for i in range(0, lax.axis_size("space"), 2)]
    zi = lax.all_gather(z_inner, "space", axis_index_groups=pairs, tiled=True)
    zo = lax.ppermute(z_outer, "space", swap("space", 1))
    ti = lax.ppermute(t_inner, "tm", swap("tm", 0))
    to = lax.ppermute(t_outer, "tm", swap("tm", 1))
    return ti, to, zi, zo


def mesh_ranks():
    return tuple(lax.axis_index(name).astype(jnp.int32).reshape(1) for name in ("tm", "space"))


def partial_rows(noise_field, gauge_links, clover, eigvecs, dilution, boundary):
    count = eigvecs.shape[0]
    noise = noise_field.reshape(-1, LANES)
    links_in = gauge_links.reshape(-1, LANES)
    clover = clover.reshape(-1, LANES)
    modes_in = eigvecs.reshape(-1, LANES)
    ranks = mesh_ranks()
    sizes = (lax.axis_size("tm"), lax.axis_size("space"))
    bits = jnp.concatenate([boundary, dilution])

    def prepare(*refs):
        prepare_kernel(sizes, *refs)

    def step_first(*refs):
        step_first_kernel(sizes, *refs)

    packed = jnp.concatenate([noise, links_in[links_in.shape[0] // 2 :]])
    sends = (packed,) * 4
    solution = None
    for iteration in range(ITERS):
        arrived = exchange(*sends)
        if iteration == 0:
            links, source = call(
                prepare,
                [jax.ShapeDtypeStruct(links_in.shape, F32), vectors(12)],
                10**6,
                (*ranks, bits),
                noise,
                links_in,
            )
            local = call(local_first_kernel, vectors(48), 5 * 10**6, (), links, clover, source)
            modes = call(
                modes_kernel,
                jax.ShapeDtypeStruct((6, 256, 256), jnp.bfloat16),
                10**6,
                (),
                modes_in,
            )
        else:
            local = call(local_kernel, vectors(48), 5 * 10**6, (), solution, links, clover, source)
        if iteration < ITERS - 1:
            first = iteration == 0
            solution, *sends = call(
                step_first if first else step_kernel,
                [vectors(48)] + [vectors(24)] * 4,
                3 * 10**6,
                (*ranks, bits) if first else ranks,
                local, links, *arrived,
                scratch=[pltpu.VMEM((12, 8, LANES), F32)] * 4 if first else (),
            )
        else:
            partial_sums = call(
                last_kernel,
                jax.ShapeDtypeStruct((32, 2 * count), F32),
                10**7,
                ranks,
                local, links, *arrived, modes,
                scratch=[pltpu.VMEM((6, 32, 256), F32)],
            )
    return partial_sums


def shards(noise_field, gauge_links, clover, eigvecs, partner, dilution, boundary):
    count = eigvecs.shape[0]
    partial_sums = partial_rows(
        noise_field, gauge_links, clover, eigvecs, dilution, boundary
    )
    both = jnp.concatenate([partner, partner + count]).reshape(1, 2 * count)
    both, partial_sums = lax.optimization_barrier((both, partial_sums))
    parts = lax.all_to_all(partial_sums, "space", 0, 0, tiled=True)
    times = lax.axis_size("tm")
    copies = call(
        sum_kernel, jax.ShapeDtypeStruct((times, 2 * count), F32), 10**4, (), parts
    )
    rows = lax.all_to_all(copies, "tm", 0, 0, tiled=True)
    row, correlator = call(
        correlate_kernel,
        [jax.ShapeDtypeStruct((1, n), F32) for n in (2 * count, times)],
        10**5,
        mesh_ranks()[:1],
        rows,
        both,
    )
    return row.reshape(1, 1, 2 * count), correlator.reshape(1, 1, times)


def solution(mesh):
    return jax.shard_map(
        shards,
        mesh=mesh,
        in_specs=(
            P(None, "tm", "space", None, None),
            P(None, None, "tm", "space", None, None),
            P(None, None, "tm", "space", None, None),
            P(None, "tm", "space", None, None),
            P(),
            P(),
            P(),
        ),
        out_specs=(P("space", "tm", None), P("space", "tm", None)),
        check_vma=False,
    )
```
